32 devices in a mesh: expert: 4 (over z), dp: 8 (over y, x, core).
Axes of the slice: x: 2, y: 2, z: 4, core: 2. Of those that a mesh axis runs over, the one named last changes fastest.
Arguments:
- tokens: bfloat16 [1024, 1408], P('dp', 'expert'), may hold values from -6 to 6
- routes: int32 [1024, 2], P('dp'), may hold values from 0 to 7, all different within a row; in each aligned block of 128 rows (0 to 127, 128 to 255, ...) at most 40 rows name the same one
- gate_values: float32 [1024, 2], P('dp'), may hold values from 0.2 to 1
- expert_in: bfloat16 [8, 1408, 6144], P('expert', None, 'dp'), may hold values from -0.15625 to 0.15625
- expert_out: bfloat16 [8, 6144, 1408], P('expert', 'dp'), may hold values from -0.078125 to 0.078125
- cotangent: bfloat16 [1024, 1408], P('dp', 'expert'), may hold values from -1.1953125 to 1.1953125
Outputs:
- layer_out: bfloat16 [1024, 1408], P('dp', 'expert')
- grad_tokens: bfloat16 [1024, 1408], P('dp', 'expert')
- grad_gates: float32 [1024, 2], P('dp')
- grad_in: bfloat16 [8, 1408, 6144], P('expert', None, 'dp')
- grad_out: bfloat16 [8, 6144, 1408], P('expert', 'dp')
The draws below stay inside these ranges and needn't reach their ends.
Inputs may be any that keep to these rules, and one draw needn't show every extreme that they name: `routes`: each row names two different experts. In each aligned block of 128 rows no expert is named by more than 40 rows, a bound that some block reaches.
All inputs are finite; a program needn't handle non-finite values.
Results may differ from the reference program's by a relative error of at most 0.014.
Values may be sent and summed in bfloat16 or wider, within the bound.
A program may use at most 128 MiB of HBM per device.

```python
import math
import jax
import jax.numpy as jnp
import numpy as np
from jax import lax

D = 1408
FF = 6144
TOK_DEV = 128
EXPERTS = 8
CAP = 40
TOKENS = 1024
N_DP = 8


def block_scale(key, shape, pieces, low, largest):
    factor_of = 1.0
    for position, shards_of in pieces:
        heights = jax.random.uniform(jax.random.fold_in(jax.random.fold_in(key, 6), position), (shards_of,), jnp.float32, low / len(pieces), largest / len(pieces))
        factor_of = factor_of * jnp.repeat(jnp.exp(heights), shape[position] // shards_of).reshape((-1,) + (1,) * (len(shape) - 1 - position))
    return factor_of


def routed_block(rng, own, number, rows, amount, top, bound, lean):
    sequence = jax.random.permutation(rng, amount)
    crowded, usual = shares(amount, rows * top, bound, lean, True), shares(amount, rows * top, bound, lean, False)
    places = jnp.arange(amount)

    def named(sizes, rotation):
        used = int((sizes > 0).sum())
        fixed = max(1, used // 4)
        moved = fixed + (places - fixed + rotation * (used - fixed)) % max(1, amount - fixed)
        return jnp.zeros((amount,), jnp.int32).at[sequence[jnp.where(places < fixed, places, moved)]].set(jnp.asarray(sizes, jnp.int32))

    sizes = jnp.where(number % 4 == 0, named(crowded, number // 4), named(usual, number - number // 4 - 1))
    mixed = jax.random.permutation(jax.random.fold_in(own, 3), amount)
    giver, sink = mixed[0:amount // 2 * 2:2], mixed[1:amount // 2 * 2:2]
    margin = jnp.minimum(sizes[giver] - 1, bound - sizes[sink]) // 2
    margin = jnp.where((giver == sequence[0]) | (sink == sequence[0]) | (sizes[sink] == 0), 0, jnp.maximum(margin, 0))
    moved = jax.random.randint(jax.random.fold_in(own, 4), (amount // 2,), 0, 1 << 20) % (margin + 1)
    sizes = sizes.at[giver].add(-moved).at[sink].add(moved)
    members = jnp.searchsorted(jnp.cumsum(sizes), jnp.arange(rows * top), side="right").astype(jnp.int32)
    table = members.reshape(top, rows).T
    table = table[jax.random.permutation(jax.random.fold_in(own, 1), rows)]
    rotation = jax.random.randint(jax.random.fold_in(own, 2), (rows, 1), 0, top)
    return jnp.take_along_axis(table, (jnp.arange(top)[None, :] + rotation) % top, axis=1)


def shares(number_of, total, most, slope, full):
    weights = [(1 << 20) // math.isqrt(rank ** slope) + 1 for rank in range(1, number_of + 1)]
    largest = most if full else min(most, max(-(-total // number_of), total * weights[0] // sum(weights)))
    least = 1 if total - largest >= number_of - 1 else 0
    counts, spare = [largest] + [least] * (number_of - 1), total - largest - least * (number_of - 1)
    while spare > 0:
        movable = [i for i in range(1, number_of) if counts[i] < largest] or [i for i in range(1, number_of) if counts[i] < most]
        whole, left = sum([weights[i] for i in movable]), spare
        for i in movable:
            more = min(most - counts[i], max(1, left * weights[i] // whole), spare)
            counts[i] = counts[i] + more
            spare = spare - more
    return np.array(counts)


def normal_values(key, extent, width, bound, shards=(), held_as=jnp.bfloat16):
    entries = width * jax.random.normal(key, extent, jnp.float32)
    if shards:
        entries = entries * block_scale(key, extent, shards, -0.22, 0.18)
    return jnp.clip(entries, -bound, bound).astype(held_as)


def setup_inputs(seed: int = 0) -> dict:
    seeds = jax.random.split(jax.random.key(seed), 7)
    tokens = normal_values(seeds[0], (TOKENS, D), 1.0, 6.0, ((0, 8), (1, 4)))
    routes_keys = jax.random.split(jax.random.fold_in(seeds[1], 1), TOKENS // TOK_DEV)
    routes_turns = jax.random.permutation(jax.random.fold_in(seeds[1], 3), TOKENS // TOK_DEV)
    routes = jax.vmap(lambda own, number: routed_block(jax.random.fold_in(seeds[1], 2), own, number, TOK_DEV, EXPERTS, 2, CAP, 2))(routes_keys, routes_turns).reshape((TOKENS, 2))
    gate_values = jnp.clip(0.2 + 0.8 * jax.random.uniform(seeds[2], (TOKENS, 2), jnp.float32) ** block_scale(seeds[2], (TOKENS, 2), ((0, 8),), -0.2, 0.2), 0.2, 1.0)
    expert_in = normal_values(seeds[3], (EXPERTS, D, FF), D ** -0.5, 0.15625, ((0, 4), (2, 8)))
    expert_out = normal_values(seeds[4], (EXPERTS, FF, D), FF ** -0.5, 0.078125, ((0, 4), (1, 8)))
    cotangent = normal_values(seeds[5], (TOKENS, D), 0.2, 1.1953125, ((0, 8), (1, 4)))
    return dict(tokens=tokens, routes=routes, gate_values=gate_values, expert_in=expert_in, expert_out=expert_out, cotangent=cotangent)


def gelu_tanh(values):
    return jax.nn.gelu(values, approximate=True)

def slot_table(routes):
    blocks = routes.reshape(N_DP, TOK_DEV * 2).astype(jnp.int32)
    onehot = (blocks[:, :, None] == jnp.arange(EXPERTS, dtype=jnp.int32)[None, None, :]).astype(jnp.int32)
    earlier = jnp.cumsum(onehot, axis=1, dtype=jnp.int32) - onehot
    rank_in = lax.optimization_barrier(jnp.sum(earlier * onehot, axis=2)).astype(jnp.int32)
    return (blocks * CAP + rank_in).astype(jnp.int32)

def place(pairs, table):

    def one_block(values, slots):
        return jnp.zeros((EXPERTS * CAP, D), jnp.bfloat16).at[slots].set(values)
    return jax.vmap(one_block)(pairs, table)

def grouped(left, right):
    rows_here = left.shape[0]
    left_parts = left.astype(jnp.float32).reshape(rows_here, N_DP, FF // N_DP)
    right_parts = right.astype(jnp.float32).reshape(N_DP, FF // N_DP, D)
    partial_sums = jnp.einsum('rgf,gfd->grd', left_parts, right_parts, precision=lax.Precision.HIGHEST)
    rounded = lax.optimization_barrier(partial_sums.astype(jnp.bfloat16))
    return lax.optimization_barrier(jnp.sum(rounded.astype(jnp.float32), axis=0)).astype(jnp.bfloat16)

def expert_pass(operands):
    x_rows, dy_rows, weight_in, weight_out = operands
    pre_act = jnp.dot(x_rows, weight_in, preferred_element_type=jnp.float32)
    hidden = gelu_tanh(pre_act).astype(jnp.bfloat16)
    d_hidden = jnp.dot(dy_rows, weight_out.T, preferred_element_type=jnp.float32)
    d_pre = jax.vjp(gelu_tanh, pre_act)[1](d_hidden)[0].astype(jnp.bfloat16)
    grad_out = jnp.dot(hidden.T, dy_rows, preferred_element_type=jnp.float32).astype(jnp.bfloat16)
    grad_in = jnp.dot(x_rows.T, d_pre, preferred_element_type=jnp.float32).astype(jnp.bfloat16)
    return (grouped(hidden, weight_out), grouped(d_pre, weight_in.T), grad_in, grad_out)

def by_expert(slots):
    return slots.reshape(N_DP, EXPERTS, CAP, D).transpose(1, 0, 2, 3).reshape(EXPERTS, N_DP * CAP, D)

def by_block(per_expert):
    return per_expert.reshape(EXPERTS, N_DP, CAP, D).transpose(1, 0, 2, 3).reshape(N_DP, EXPERTS * CAP, D)

def pick(arrays, table):
    return jax.vmap(lambda block, slots: block[slots])(arrays, table)

def reference(tokens, routes, gate_values, expert_in, expert_out, cotangent):
    table = slot_table(routes)
    gates = gate_values.reshape(N_DP, TOK_DEV * 2).astype(jnp.float32)
    pair_x = jnp.repeat(tokens.reshape(N_DP, TOK_DEV, D), 2, axis=1)
    cot_blocks = cotangent.reshape(N_DP, TOK_DEV, D).astype(jnp.float32)
    pair_dy = (jnp.repeat(cot_blocks, 2, axis=1) * gates[:, :, None]).astype(jnp.bfloat16)
    outputs, input_grads, grad_in, grad_out = lax.map(expert_pass, (by_expert(place(pair_x, table)), by_expert(place(pair_dy, table)), expert_in, expert_out))
    out_pairs = pick(by_block(outputs), table).astype(jnp.float32).reshape(N_DP, TOK_DEV, 2, D)
    dx_pairs = pick(by_block(input_grads), table).astype(jnp.float32).reshape(N_DP, TOK_DEV, 2, D)
    gate_view = gates.reshape(N_DP, TOK_DEV, 2)
    layer_out = out_pairs[:, :, 0] * gate_view[:, :, 0:1] + out_pairs[:, :, 1] * gate_view[:, :, 1:2]
    layer_out = layer_out.astype(jnp.bfloat16).reshape(TOKENS, D)
    grad_tokens = (dx_pairs[:, :, 0] + dx_pairs[:, :, 1]).astype(jnp.bfloat16).reshape(TOKENS, D)
    grad_gates = lax.optimization_barrier(jnp.sum(cot_blocks[:, :, None, :] * out_pairs, axis=3)).reshape(TOKENS, 2)
    return (layer_out, grad_tokens, grad_gates, grad_in, grad_out)
```

```python
import jax
import jax.numpy as jnp
from jax import lax
from jax.experimental import pallas as pl
from jax.experimental.pallas import tpu as pltpu
from jax.sharding import PartitionSpec as P


def gelu_tanh(values):
    return jax.nn.gelu(values, approximate=True)


def shards(tokens, routes, gate_values, expert_in, expert_out, cotangent):
    tok_dev, columns = tokens.shape
    groups = lax.axis_size("expert")
    per_dev = expert_in.shape[0]
    experts = per_dev * groups
    capacity = 5 * tok_dev // (2 * experts)
    full_width = columns * groups
    slot_rows = per_dev * capacity
    slot_count = experts * capacity
    flat_routes = routes.reshape(-1)
    pairs_here = flat_routes.shape[0]
    places = jnp.arange(pairs_here, dtype=jnp.int32)
    same = flat_routes[:, None] == flat_routes[None, :]
    rank_in = jnp.sum((same & (places[None, :] < places[:, None])).astype(jnp.int32), axis=1)
    owner_idx = flat_routes // per_dev
    within = flat_routes % per_dev
    slot_ids = (within * capacity + rank_in) * groups + owner_idx
    placing = (slot_ids[:, None] == jnp.arange(slot_count, dtype=jnp.int32)[None, :]).astype(
        jnp.bfloat16
    )
    pair_gates = gate_values.reshape(-1)
    pair_tokens = jnp.repeat(tokens, 2, axis=0)
    cot_float = cotangent.astype(jnp.float32)
    pair_cot = (jnp.repeat(cot_float, 2, axis=0) * pair_gates[:, None]).astype(jnp.bfloat16)

    def to_slots(pairs):
        slots = jnp.einsum("ps,pc->sc", placing, pairs, preferred_element_type=jnp.float32)
        return slots.astype(jnp.bfloat16).reshape(slot_rows, groups, columns)

    def from_slots(back):
        return jnp.einsum(
            "ps,sc->pc",
            placing,
            back.reshape(slot_count, columns),
            preferred_element_type=jnp.float32,
        )

    def as_rows(gathered):
        return gathered.reshape(-1, per_dev, capacity, full_width)

    x_moved = lax.all_to_all(
        to_slots(pair_tokens), "expert", split_axis=1, concat_axis=1, tiled=True
    )
    x_rows = as_rows(
        lax.all_gather(x_moved.reshape(slot_rows, full_width), "dp", axis=0, tiled=True)
    )
    pre_act = jnp.einsum("bjcd,jdf->bjcf", x_rows, expert_in, preferred_element_type=jnp.float32)
    pre_act, hidden = (pre_act, gelu_tanh(pre_act).astype(jnp.bfloat16))
    part = hidden
    term = jnp.einsum("bjcf,jfd->bjcd", part, expert_out, preferred_element_type=jnp.float32)
    out_sum = lax.psum_scatter(
        term.reshape(lax.axis_size("dp") * slot_rows, full_width).astype(jnp.bfloat16),
        "dp",
        scatter_dimension=0,
        tiled=True,
    )
    out_back = lax.all_to_all(
        out_sum.reshape(slot_rows, groups, columns),
        "expert",
        split_axis=1,
        concat_axis=1,
        tiled=True,
    )
    dy_moved = lax.all_to_all(to_slots(pair_cot), "expert", split_axis=1, concat_axis=1, tiled=True)
    dy_rows = as_rows(
        lax.all_gather(dy_moved.reshape(slot_rows, full_width), "dp", axis=0, tiled=True)
    )
    d_hidden = jnp.einsum("bjcd,jfd->bjcf", dy_rows, expert_out, preferred_element_type=jnp.float32)
    backward_d_pre = jax.vjp(gelu_tanh, pre_act)[1](d_hidden)[0].astype(jnp.bfloat16)
    grad_out = jnp.einsum("bjcf,bjcd->jfd", hidden, dy_rows, preferred_element_type=jnp.float32)
    grad_in = jnp.einsum(
        "bjcd,bjcf->jdf", x_rows, backward_d_pre, preferred_element_type=jnp.float32
    )
    d_pre, grad_in, grad_out = (
        backward_d_pre,
        grad_in.astype(jnp.bfloat16),
        grad_out.astype(jnp.bfloat16),
    )
    part = d_pre
    term = jnp.einsum("bjcf,jdf->bjcd", part, expert_in, preferred_element_type=jnp.float32)
    dx_sum = lax.psum_scatter(
        term.reshape(lax.axis_size("dp") * slot_rows, full_width).astype(jnp.bfloat16),
        "dp",
        scatter_dimension=0,
        tiled=True,
    )
    dx_back = lax.all_to_all(
        dx_sum.reshape(slot_rows, groups, columns),
        "expert",
        split_axis=1,
        concat_axis=1,
        tiled=True,
    )
    out_view = from_slots(out_back).reshape(tok_dev, 2, columns)
    dx_view = from_slots(dx_back).reshape(tok_dev, 2, columns)
    gate_pairs = pair_gates.reshape(tok_dev, 2)
    layer_out = (out_view[:, 0] * gate_pairs[:, 0:1] + out_view[:, 1] * gate_pairs[:, 1:2]).astype(
        jnp.bfloat16
    )
    grad_tokens = (dx_view[:, 0] + dx_view[:, 1]).astype(jnp.bfloat16)
    gate_part = jnp.sum(cot_float[:, None, :] * out_view, axis=2)
    grad_gates = lax.psum(gate_part, "expert")
    return (layer_out, grad_tokens, grad_gates, grad_in, grad_out)


MESH = pl.DeviceIdType.MESH
BF16 = jnp.bfloat16
F32 = jnp.float32


def tiles_of(lo, hi, step=256):
    return [(at, min(at + step, hi)) for at in range(lo, hi, step)]


def dot(left, right, contract):
    return lax.dot_general(left, right, ((contract[:1], contract[1:]), ((), ())), preferred_element_type=F32)


def layer_kernel(
    tok_ref, cot_ref, routes_t, gates_t, w_in_hbm, w_out_hbm,
    out_ref, gtok_ref, gg_ref, gi, go,
    w_in, w_out, slots, zgot, own, rest, rows, hid, slope, dpre,
    term_o, mate_o, sums_o, relay_o, land_o,
    term_r, mate_r, sums_r, relay_r, land_r,
    term_w, mate_w, sums_w, relay_w, land_w,
    zsend_o, zsend_r, zback, place, gpart,
    wsem, a2a_s, a2a_r, own_s, own_r, rest_s, rest_r, mates_s, mates_r, rs_s, rs_r, back_s, back_r, gg_s, gg_r,
):
    cols, tok_dev = tok_ref.shape
    zs, per_dev, cap = slots.shape[1:4]
    width, hidden_here = w_in.shape[1:]
    others = width - cols
    experts = zs * per_dev
    z = lax.axis_index("expert")
    d = lax.axis_index("dp")
    core = d % 2
    xbit = (d // 2) % 2
    ybit = d // 4
    mate_d = d + 1 - 2 * core
    xn = d + 2 - 4 * xbit
    yn = d + 4 - 8 * ybit
    dd = xn + 4 - 8 * ybit
    first = core * yn + (1 - core) * xn
    second = core * xn + (1 - core) * yn

    def remote(src, dst, send, recv, zi, di):
        return pltpu.make_async_remote_copy(
            src_ref=src, dst_ref=dst, send_sem=send, recv_sem=recv, device_id=(zi, di), device_id_type=MESH
        )

    barrier = pltpu.get_barrier_semaphore()
    for step in range(1, zs):
        pl.semaphore_signal(barrier, inc=1, device_id=((z + step) % zs, d), device_id_type=MESH)
    for other in (mate_d, xn, yn):
        pl.semaphore_signal(barrier, inc=1, device_id=(z, other), device_id_type=MESH)

    w_copies = []
    for j in range(per_dev):
        for i in range(zs):
            piece = pl.ds(pl.multiple_of(((z + i) % zs) * cols, 16), cols)
            w_copies.append(
                pltpu.make_async_copy(
                    w_in_hbm.at[j, piece], w_in.at[j, i * cols : (i + 1) * cols], wsem.at[j, i]
                )
            )
    for j in range(per_dev):
        w_copies.append(pltpu.make_async_copy(w_out_hbm.at[j], w_out.at[j], wsem.at[j, zs]))
    for copy in w_copies:
        copy.start()

    named = lax.broadcasted_iota(jnp.int32, (experts, tok_dev), 0)
    first_of = (named == routes_t[0:1, :]).astype(F32)
    second_of = (named == routes_t[1:2, :]).astype(F32)
    before = (
        lax.broadcasted_iota(jnp.int32, (tok_dev, tok_dev), 0)
        < lax.broadcasted_iota(jnp.int32, (tok_dev, tok_dev), 1)
    ).astype(F32).astype(BF16)
    earlier = dot((first_of + second_of).astype(BF16), before, (1, 0))
    slot_iota = lax.broadcasted_iota(jnp.int32, (experts * cap, tok_dev), 0)
    gate_col = jnp.zeros((experts * cap, 1), F32)
    for k, of in ((0, first_of), (1, second_of)):
        rank = jnp.sum(earlier * of, axis=0, keepdims=True).astype(jnp.int32)
        taken = (slot_iota == routes_t[k : k + 1, :] * cap + rank).astype(F32)
        place[k] = taken.astype(BF16)
        gate_col = gate_col + jnp.sum(taken * gates_t[k : k + 1, :], axis=1, keepdims=True)
    both = place[0] + place[1]
    by_slot = (zs, per_dev, cap, cols)

    a2a = [
        [
            [
                remote(
                    slots.at[a, (z + step) % zs, j], zgot.at[a, z, j],
                    a2a_s.at[a, j, step - 1], a2a_r.at[a, j, step - 1], (z + step) % zs, d,
                )
                for step in range(1, zs)
            ]
            for j in range(per_dev)
        ]
        for a in range(2)
    ]

    def exchange(a, j):
        for copy in a2a[a][j]:
            copy.start()

    def arrive(a, j):
        for copy in a2a[a][j]:
            copy.wait()

    def ag_copies(at, send, recv):
        made = []
        for i, (block, to) in enumerate(
            ((d, xn), (d, yn), (d, mate_d), (second, first), (xn, mate_d), (yn, mate_d), (dd, mate_d))
        ):
            made.append(remote(at(block), at(block), send.at[i], recv.at[i], z, to))
        return made

    ag_own = [ag_copies(lambda b, a=a: own.at[a, b], own_s.at[a], own_r.at[a]) for a in range(2)]
    ag_rest = [
        [
            ag_copies(lambda b, a=a, j=j: rest.at[a, j, b], rest_s.at[a, j], rest_r.at[a, j])
            for j in range(per_dev)
        ]
        for a in range(2)
    ]

    def own_start(a):
        own[a, pl.ds(d, 1)] = slots[a, pl.ds(z, 1)]
        for copy in ag_own[a][:3]:
            copy.start()

    def assemble(a, j):
        whole = jnp.concatenate([zgot[a, (z + i) % zs, j].astype(F32) for i in range(1, zs)], axis=-1)
        rest[a, j, pl.ds(d, 1)] = whole.astype(BF16)[None]
        for copy in ag_rest[a][j][:3]:
            copy.start()

    def forward(copies):
        copies[0].wait_recv()
        copies[1].wait_recv()
        for i in (3, 4, 5):
            copies[i].start()

    def forward_last(copies):
        copies[3].wait_recv()
        copies[6].start()

    def landed_all(copies):
        for i in (2, 4, 5, 6):
            copies[i].wait_recv()

    chips = rows.shape[2] // (2 * cap)

    def finish(a, j, order):
        def pair(n, carry):
            half = n // (chips // 2)
            chip = (n % (chips // 2)) * 2
            blocks = []
            for b in (2 * chip + half, 2 * chip + 2 + half):
                mine = own[a, b, j].astype(F32)
                far = rest[a, j, b].astype(F32)
                pieces = [mine if i == 0 else far[:, (i - 1) * cols : i * cols] for i in order]
                blocks.append(jnp.concatenate(pieces, axis=-1))
            at = pl.ds(pl.multiple_of(n * 2 * cap, 2 * cap), 2 * cap)
            rows[a, j, at, :] = jnp.concatenate(blocks, axis=0).astype(BF16)
            return carry

        lax.fori_loop(0, chips, pair, 0)

    def finish_x(j):
        landed_all(ag_rest[0][j])
        finish(0, j, list(range(zs)))

    def finish_dy(j):
        landed_all(ag_rest[1][j])
        for here in range(zs):

            @pl.when(z == here)
            def _():
                finish(1, j, [(p - here) % zs for p in range(zs)])

    def activation(j, lo, hi):
        for start, end in tiles_of(lo, hi):
            v = dot(rows[0, j], w_in[j, :, start:end], (1, 0))
            scale = 0.7978845608028654
            sq = v * v
            t = jnp.tanh(scale * v * (1.0 + 0.044715 * sq))
            half = 0.5 * (1.0 + t)
            hid[j, :, start:end] = (v * half).astype(BF16)
            slope[j, :, start:end] = half + 0.5 * v * (1.0 - t * t) * (scale * (1.0 + 0.134145 * sq))

    def backward(j, lo, hi):
        for start, end in tiles_of(lo, hi):
            dh = dot(rows[1, j], w_out[j, start:end, :], (1, 1))
            dpre[j, :, start:end] = (slope[j, :, start:end] * dh).astype(BF16)

    class Scatter:
        def __init__(self, index, term, mate, sums, relay, land):
            self.term, self.sums, self.relay, self.land, self.mate_ref = term, sums, relay, land, mate
            self.mate = remote(term.at[1 - core], mate, mates_s.at[index], mates_r.at[index], z, mate_d)
            self.hops = [
                remote(src, land.at[i], rs_s.at[index, i], rs_r.at[index, i], z, to)
                for i, (src, to) in enumerate(
                    ((sums.at[dd // 2], first), (sums.at[first // 2], first), (relay, second))
                )
            ]

        def swap(self):
            self.mate.start()

        def start(self):
            self.mate.wait()

            def chip(c, carry):
                both_cores = self.term[core, c].astype(F32) + self.mate_ref[c].astype(F32)
                self.sums[c] = both_cores.astype(BF16)
                return carry

            lax.fori_loop(0, chips, chip, 0)
            self.hops[0].start()
            self.hops[1].start()

        def pass_on(self):
            self.hops[0].wait()
            self.relay[...] = (self.sums[second // 2].astype(F32) + self.land[0].astype(F32)).astype(BF16)
            self.hops[2].start()

        def end(self):
            self.hops[1].wait()
            self.hops[2].wait()
            return self.sums[d // 2].astype(F32) + self.land[1].astype(F32) + self.land[2].astype(F32)

    rs_out = [
        Scatter(j, term_o.at[j], mate_o.at[j], sums_o.at[j], relay_o.at[j], land_o.at[j])
        for j in range(per_dev)
    ]
    rs_rest = [
        Scatter(per_dev + j, term_r.at[j], mate_r.at[j], sums_r.at[j], relay_r.at[j], land_r.at[j])
        for j in range(per_dev)
    ]
    rs_own = Scatter(2 * per_dev, term_w, mate_w, sums_w, relay_w, land_w)

    def terms_out(j):
        for lo, hi in tiles_of(0, width):
            v = dot(hid[j], w_out[j, :, lo:hi], (1, 0))
            term_o[j, :, :, :, lo:hi] = v.reshape(2, chips, cap, hi - lo).astype(BF16)
        rs_out[j].swap()

    def terms_rest(j):
        for lo, hi in tiles_of(0, others):
            v = dot(dpre[j], w_in[j, cols + lo : cols + hi, :], (1, 1))
            term_r[j, :, :, :, lo:hi] = v.reshape(2, chips, cap, hi - lo).astype(BF16)
        rs_rest[j].swap()

    def terms_own(j):
        v = dot(dpre[j], w_in[j, 0:cols, :], (1, 1))
        term_w[:, :, j] = v.reshape(2, chips, cap, cols).astype(BF16)

    back_o = [
        [
            remote(
                zsend_o.at[(z + step) % zs, j], zback.at[0, z, j],
                back_s.at[0, j, step - 1], back_r.at[0, j, step - 1], (z + step) % zs, d,
            )
            for step in range(1, zs)
        ]
        for j in range(per_dev)
    ]
    back_x = [
        [
            remote(
                zsend_r.at[step - 1, j], zback.at[1, z, j],
                back_s.at[1, j, step - 1], back_r.at[1, j, step - 1], (z + step) % zs, d,
            )
            for step in range(1, zs)
        ]
        for j in range(per_dev)
    ]

    def end_out(j):
        total = rs_out[j].end()
        for i in range(zs):
            zsend_o[i, j] = total[:, i * cols : (i + 1) * cols].astype(BF16)
        for copy in back_o[j]:
            copy.start()
        zback[0, pl.ds(z, 1), j] = zsend_o[pl.ds(z, 1), j]

    def end_rest(j):
        total = rs_rest[j].end()
        for i in range(zs - 1):
            zsend_r[i, j] = total[:, i * cols : (i + 1) * cols].astype(BF16)
        for copy in back_x[j]:
            copy.start()

    def end_own():
        zback[1, pl.ds(z, 1)] = rs_own.end().astype(BF16)[None]

    def weight_grad_out(j, lo, hi):
        for start, end in tiles_of(lo, hi):
            go[j, start:end, :] = dot(hid[j, :, start:end], rows[1, j], (0, 0)).astype(BF16)

    def weight_grad_in(j, lo, hi):
        for start, end in tiles_of(lo, hi):
            gi[j, start:end, :] = dot(rows[0, j, :, start:end], dpre[j], (0, 0)).astype(BF16)

    gg = []
    for step in range(1, zs):
        gg.append(
            remote(
                gpart.at[z], gpart.at[z], gg_s.at[step - 1], gg_r.at[step - 1], (z + step) % zs, d
            )
        )

    def views_of(a):
        slot_rows = zback[a].astype(F32).reshape(experts * cap, cols).astype(BF16)
        return [dot(slot_rows, place[k], (0, 0)) for k in range(2)]

    def combine_out():
        for j in range(per_dev):
            for copy in back_o[j]:
                copy.wait()
        views = views_of(0)
        out_ref[...] = (views[0] * gates_t[0:1, :] + views[1] * gates_t[1:2, :]).astype(BF16)
        cot = cot_ref[...].astype(F32)
        inner = [jnp.sum(cot * v, axis=0, keepdims=True) for v in views]
        row = lax.broadcasted_iota(jnp.int32, (8, tok_dev), 0)
        gpart[pl.ds(z, 1)] = jnp.where(row == 0, inner[0], inner[1])[None]
        for copy in gg:
            copy.start()

    def combine_tok():
        for j in range(per_dev):
            for copy in back_x[j]:
                copy.wait()
        views = views_of(1)
        gtok_ref[...] = (views[0] + views[1]).astype(BF16)

    slots[0] = dot(both, tok_ref[...], (1, 1)).reshape(by_slot).astype(BF16)
    pl.semaphore_wait(barrier, zs + 2)
    exchange(0, 0)
    own_start(0)
    exchange(0, 1)
    slots[1] = (dot(both, cot_ref[...], (1, 1)) * gate_col).reshape(by_slot).astype(BF16)
    own_start(1)
    forward(ag_own[0])
    arrive(0, 0)
    assemble(0, 0)
    exchange(1, 0)
    forward(ag_own[1])
    forward_last(ag_own[0])
    arrive(0, 1)
    assemble(0, 1)
    exchange(1, 1)
    forward_last(ag_own[1])
    forward(ag_rest[0][0])
    arrive(1, 0)
    assemble(1, 0)
    forward(ag_rest[0][1])
    forward_last(ag_rest[0][0])
    for copy in w_copies:
        copy.wait()
    landed_all(ag_own[0])
    finish_x(0)
    activation(0, 0, 256)
    arrive(1, 1)
    assemble(1, 1)
    activation(0, 256, hidden_here)
    forward_last(ag_rest[0][1])
    forward(ag_rest[1][0])
    terms_out(0)
    finish_x(1)
    activation(1, 0, 512)
    forward(ag_rest[1][1])
    forward_last(ag_rest[1][0])
    rs_out[0].start()
    activation(1, 512, hidden_here)
    terms_out(1)
    forward_last(ag_rest[1][1])
    landed_all(ag_own[1])
    finish_dy(0)
    rs_out[1].start()
    backward(0, 0, hidden_here)
    terms_rest(0)
    rs_out[0].pass_on()
    finish_dy(1)
    backward(1, 0, hidden_here)
    rs_rest[0].start()
    terms_rest(1)
    terms_own(0)
    terms_own(1)
    rs_own.swap()
    weight_grad_out(0, 0, 256)
    rs_out[1].pass_on()
    end_out(0)
    rs_rest[1].start()
    rs_own.start()
    weight_grad_out(0, 256, hidden_here)
    weight_grad_out(1, 0, 256)
    rs_rest[0].pass_on()
    end_out(1)
    weight_grad_out(1, 256, hidden_here)
    weight_grad_in(0, 0, 512)
    rs_rest[1].pass_on()
    end_rest(0)
    weight_grad_in(0, 512, width)
    rs_own.pass_on()
    end_rest(1)
    combine_out()
    weight_grad_in(1, 0, width)
    for copy in gg:
        copy.wait()
    total = gpart[0] + gpart[1] + gpart[2] + gpart[3]
    gg_ref[...] = total[0:2]
    end_own()
    combine_tok()
    for a in range(2):
        for copy in ag_own[a]:
            copy.wait_send()
        for j in range(per_dev):
            for copy in ag_rest[a][j]:
                copy.wait_send()


def store_kernel(out_in, gtok_in, gg_in, gi, go, out_hbm, gtok_hbm, gg_hbm, gi_hbm, go_hbm, sem, wsem):
    per_dev, width, _ = gi.shape
    zs = wsem.shape[1] - 1
    cols = width // zs
    z = lax.axis_index("expert")
    copies = []
    for j in range(per_dev):
        copies.append(pltpu.make_async_copy(go.at[j], go_hbm.at[j], wsem.at[j, zs]))
        for i in range(zs):
            piece = pl.ds(pl.multiple_of(((z + i) % zs) * cols, 16), cols)
            copies.append(
                pltpu.make_async_copy(gi.at[j, i * cols : (i + 1) * cols], gi_hbm.at[j, piece], wsem.at[j, i])
            )
    for i, (here, there) in enumerate(((out_in, out_hbm), (gtok_in, gtok_hbm), (gg_in, gg_hbm))):
        copies.append(pltpu.make_async_copy(here, there, sem.at[i]))
    for copy in copies:
        copy.start()
    for copy in copies:
        copy.wait()


def fused_shards(tokens, routes, gate_values, expert_in, expert_out, cotangent):
    tok_dev, cols = tokens.shape
    zs = lax.axis_size("expert")
    dps = lax.axis_size("dp")
    per_dev, width, hidden_here = expert_in.shape
    experts = per_dev * zs
    cap = 5 * tok_dev // (2 * experts)
    all_rows = dps * cap
    others = width - cols
    chips = dps // 2
    vmem = pl.BlockSpec(memory_space=pltpu.VMEM)
    hbm = pl.BlockSpec(memory_space=pl.ANY)
    dma = pltpu.SemaphoreType.DMA

    def scatter_buffers(lead, tail):
        return [
            pltpu.VMEM(lead + (2, chips) + tail, BF16),
            pltpu.VMEM(lead + (chips,) + tail, BF16),
            pltpu.VMEM(lead + (chips,) + tail, BF16),
            pltpu.VMEM(lead + tail, BF16),
            pltpu.VMEM(lead + (3,) + tail, BF16),
        ]

    groups = 2 * per_dev + 1
    results = pl.pallas_call(
        layer_kernel,
        out_shape=(
            pltpu.VMEM((cols, tok_dev), BF16),
            pltpu.VMEM((cols, tok_dev), BF16),
            pltpu.VMEM((2, tok_dev), F32),
            pltpu.VMEM(expert_in.shape, BF16),
            pltpu.VMEM(expert_out.shape, BF16),
        ),
        in_specs=[vmem] * 4 + [hbm] * 2,
        out_specs=(vmem,) * 5,
        scratch_shapes=[
            pltpu.VMEM(expert_in.shape, BF16),
            pltpu.VMEM(expert_out.shape, BF16),
            pltpu.VMEM((2, zs, per_dev, cap, cols), BF16),
            pltpu.VMEM((2, zs, per_dev, cap, cols), BF16),
            pltpu.VMEM((2, dps, per_dev, cap, cols), BF16),
            pltpu.VMEM((2, per_dev, dps, cap, others), BF16),
            pltpu.VMEM((2, per_dev, all_rows, width), BF16),
            pltpu.VMEM((per_dev, all_rows, hidden_here), BF16),
            pltpu.VMEM((per_dev, all_rows, hidden_here), F32),
            pltpu.VMEM((per_dev, all_rows, hidden_here), BF16),
            *scatter_buffers((per_dev,), (cap, width)),
            *scatter_buffers((per_dev,), (cap, others)),
            *scatter_buffers((), (per_dev, cap, cols)),
            pltpu.VMEM((zs, per_dev, cap, cols), BF16),
            pltpu.VMEM((zs - 1, per_dev, cap, cols), BF16),
            pltpu.VMEM((2, zs, per_dev, cap, cols), BF16),
            pltpu.VMEM((2, experts * cap, tok_dev), BF16),
            pltpu.VMEM((zs, 8, tok_dev), F32),
            dma((per_dev, zs + 1)),
            dma((2, per_dev, zs - 1)), dma((2, per_dev, zs - 1)),
            dma((2, 7)), dma((2, 7)),
            dma((2, per_dev, 7)), dma((2, per_dev, 7)),
            dma((groups,)), dma((groups,)),
            dma((groups, 3)), dma((groups, 3)),
            dma((2, per_dev, zs - 1)), dma((2, per_dev, zs - 1)),
            dma((zs - 1,)), dma((zs - 1,)),
        ],
        compiler_params=pltpu.CompilerParams(
            collective_id=0, has_side_effects=True, vmem_limit_bytes=48 * 1024 * 1024
        ),
    )(tokens.T, cotangent.T, routes.T, gate_values.T, expert_in, expert_out)
    layer_t, gtok_t, gates_grad_t, grad_in, grad_out = pl.pallas_call(
        store_kernel,
        out_shape=(
            jax.ShapeDtypeStruct((cols, tok_dev), BF16),
            jax.ShapeDtypeStruct((cols, tok_dev), BF16),
            jax.ShapeDtypeStruct((2, tok_dev), F32),
            jax.ShapeDtypeStruct(expert_in.shape, BF16),
            jax.ShapeDtypeStruct(expert_out.shape, BF16),
        ),
        in_specs=[vmem] * 5,
        out_specs=(hbm,) * 5,
        scratch_shapes=[dma((3,)), dma((per_dev, zs + 1))],
        compiler_params=pltpu.CompilerParams(vmem_limit_bytes=1024 * 1024),
    )(*results)
    return (layer_t.T, gtok_t.T, gates_grad_t.T, grad_in, grad_out)


def solution(mesh):
    placed = (
        P("dp", "expert"),
        P("dp", None),
        P("dp", None),
        P("expert", None, "dp"),
        P("expert", "dp", None),
        P("dp", "expert"),
    )
    fused = mesh.shape["expert"] == 4 and mesh.shape["dp"] == 8
    return jax.shard_map(
        fused_shards if fused else shards,
        mesh=mesh,
        in_specs=placed,
        out_specs=(
            P("dp", "expert"),
            P("dp", "expert"),
            P("dp", None),
            P("expert", None, "dp"),
            P("expert", "dp", None),
        ),
        check_vma=False,
    )
```

```python
import jax
import jax.numpy as jnp
from jax import lax
from jax.experimental import pallas as pl
from jax.experimental.pallas import tpu as pltpu
from jax.sharding import PartitionSpec as P


def gelu_tanh(values):
    return jax.nn.gelu(values, approximate=True)


def shards(tokens, routes, gate_values, expert_in, expert_out, cotangent):
    tok_dev, columns = tokens.shape
    groups = lax.axis_size("expert")
    per_dev = expert_in.shape[0]
    experts = per_dev * groups
    capacity = 5 * tok_dev // (2 * experts)
    full_width = columns * groups
    slot_rows = per_dev * capacity
    slot_count = experts * capacity
    flat_routes = routes.reshape(-1)
    pairs_here = flat_routes.shape[0]
    places = jnp.arange(pairs_here, dtype=jnp.int32)
    same = flat_routes[:, None] == flat_routes[None, :]
    rank_in = jnp.sum((same & (places[None, :] < places[:, None])).astype(jnp.int32), axis=1)
    owner_idx = flat_routes // per_dev
    within = flat_routes % per_dev
    slot_ids = (within * capacity + rank_in) * groups + owner_idx
    placing = (slot_ids[:, None] == jnp.arange(slot_count, dtype=jnp.int32)[None, :]).astype(
        jnp.bfloat16
    )
    pair_gates = gate_values.reshape(-1)
    pair_tokens = jnp.repeat(tokens, 2, axis=0)
    cot_float = cotangent.astype(jnp.float32)
    pair_cot = (jnp.repeat(cot_float, 2, axis=0) * pair_gates[:, None]).astype(jnp.bfloat16)

    def to_slots(pairs):
        slots = jnp.einsum("ps,pc->sc", placing, pairs, preferred_element_type=jnp.float32)
        return slots.astype(jnp.bfloat16).reshape(slot_rows, groups, columns)

    def from_slots(back):
        return jnp.einsum(
            "ps,sc->pc",
            placing,
            back.reshape(slot_count, columns),
            preferred_element_type=jnp.float32,
        )

    def as_rows(gathered):
        return gathered.reshape(-1, per_dev, capacity, full_width)

    x_moved = lax.all_to_all(
        to_slots(pair_tokens), "expert", split_axis=1, concat_axis=1, tiled=True
    )
    x_rows = as_rows(
        lax.all_gather(x_moved.reshape(slot_rows, full_width), "dp", axis=0, tiled=True)
    )
    pre_act = jnp.einsum("bjcd,jdf->bjcf", x_rows, expert_in, preferred_element_type=jnp.float32)
    pre_act, hidden = (pre_act, gelu_tanh(pre_act).astype(jnp.bfloat16))
    part = hidden
    term = jnp.einsum("bjcf,jfd->bjcd", part, expert_out, preferred_element_type=jnp.float32)
    out_sum = lax.psum_scatter(
        term.reshape(lax.axis_size("dp") * slot_rows, full_width).astype(jnp.bfloat16),
        "dp",
        scatter_dimension=0,
        tiled=True,
    )
    out_back = lax.all_to_all(
        out_sum.reshape(slot_rows, groups, columns),
        "expert",
        split_axis=1,
        concat_axis=1,
        tiled=True,
    )
    dy_moved = lax.all_to_all(to_slots(pair_cot), "expert", split_axis=1, concat_axis=1, tiled=True)
    dy_rows = as_rows(
        lax.all_gather(dy_moved.reshape(slot_rows, full_width), "dp", axis=0, tiled=True)
    )
    d_hidden = jnp.einsum("bjcd,jfd->bjcf", dy_rows, expert_out, preferred_element_type=jnp.float32)
    backward_d_pre = jax.vjp(gelu_tanh, pre_act)[1](d_hidden)[0].astype(jnp.bfloat16)
    grad_out = jnp.einsum("bjcf,bjcd->jfd", hidden, dy_rows, preferred_element_type=jnp.float32)
    grad_in = jnp.einsum(
        "bjcd,bjcf->jdf", x_rows, backward_d_pre, preferred_element_type=jnp.float32
    )
    d_pre, grad_in, grad_out = (
        backward_d_pre,
        grad_in.astype(jnp.bfloat16),
        grad_out.astype(jnp.bfloat16),
    )
    part = d_pre
    term = jnp.einsum("bjcf,jdf->bjcd", part, expert_in, preferred_element_type=jnp.float32)
    dx_sum = lax.psum_scatter(
        term.reshape(lax.axis_size("dp") * slot_rows, full_width).astype(jnp.bfloat16),
        "dp",
        scatter_dimension=0,
        tiled=True,
    )
    dx_back = lax.all_to_all(
        dx_sum.reshape(slot_rows, groups, columns),
        "expert",
        split_axis=1,
        concat_axis=1,
        tiled=True,
    )
    out_view = from_slots(out_back).reshape(tok_dev, 2, columns)
    dx_view = from_slots(dx_back).reshape(tok_dev, 2, columns)
    gate_pairs = pair_gates.reshape(tok_dev, 2)
    layer_out = (out_view[:, 0] * gate_pairs[:, 0:1] + out_view[:, 1] * gate_pairs[:, 1:2]).astype(
        jnp.bfloat16
    )
    grad_tokens = (dx_view[:, 0] + dx_view[:, 1]).astype(jnp.bfloat16)
    gate_part = jnp.sum(cot_float[:, None, :] * out_view, axis=2)
    grad_gates = lax.psum(gate_part, "expert")
    return (layer_out, grad_tokens, grad_gates, grad_in, grad_out)


MESH = pl.DeviceIdType.MESH
BF16 = jnp.bfloat16
F32 = jnp.float32


def tiles_of(lo, hi, step=256):
    return [(at, min(at + step, hi)) for at in range(lo, hi, step)]


def dot(left, right, contract):
    return lax.dot_general(left, right, ((contract[:1], contract[1:]), ((), ())), preferred_element_type=F32)


def layer_kernel(
    tok_hbm, cot_hbm, routes_hbm, gates_hbm, w_in_hbm, w_out_hbm,
    out_ref, gtok_ref, gg_ref, gi, go,
    tok_ref, cot_ref, routes_t, gates_t,
    w_in, w_out, slots, zgot, own, rest, rows, hid, slope, dpre,
    term, mate, sums_r, relay_r, land_r, sums_w, relay_w, land_w, tails, zsend, zback, place, gpart,
    isem, wsem, a2a_s, a2a_r, own_s, own_r, rest_s, rest_r, mates_s, mates_r, rs_s, rs_r, rsw_s, rsw_r,
    back_s, back_r, gg_s, gg_r,
):
    cols, tok_dev = tok_ref.shape
    zs, per_dev, cap = slots.shape[1:4]
    width, hidden_here = w_in.shape[1:]
    head = own.shape[-1]
    experts = zs * per_dev
    z = lax.axis_index("expert")
    d = lax.axis_index("dp")
    core = d % 2
    xbit = (d // 2) % 2
    ybit = d // 4
    mate_d = d + 1 - 2 * core
    xn = d + 2 - 4 * xbit
    yn = d + 4 - 8 * ybit
    dd = xn + 4 - 8 * ybit
    first = core * yn + (1 - core) * xn
    second = core * xn + (1 - core) * yn

    def remote(src, dst, send, recv, zi, di):
        return pltpu.make_async_remote_copy(
            src_ref=src, dst_ref=dst, send_sem=send, recv_sem=recv, device_id=(zi, di), device_id_type=MESH
        )

    loads = [
        pltpu.make_async_copy(src, dst, isem.at[i])
        for i, (src, dst) in enumerate(
            ((routes_hbm, routes_t), (tok_hbm, tok_ref), (gates_hbm, gates_t), (cot_hbm, cot_ref))
        )
    ]
    for copy in loads:
        copy.start()
    barrier = pltpu.get_barrier_semaphore()
    for step in range(1, zs):
        pl.semaphore_signal(barrier, inc=1, device_id=((z + step) % zs, d), device_id_type=MESH)
    for other in (mate_d, xn, yn):
        pl.semaphore_signal(barrier, inc=1, device_id=(z, other), device_id_type=MESH)

    w_copies = []
    for j in range(per_dev):
        for i in range(zs):
            piece = pl.ds(pl.multiple_of(((z + i) % zs) * cols, 16), cols)
            w_copies.append(
                pltpu.make_async_copy(
                    w_in_hbm.at[j, piece], w_in.at[j, i * cols : (i + 1) * cols], wsem.at[j, i]
                )
            )
    for j in range(per_dev):
        w_copies.append(pltpu.make_async_copy(w_out_hbm.at[j], w_out.at[j], wsem.at[j, zs]))
    for copy in w_copies:
        copy.start()

    for copy in (loads[0], loads[2], loads[1], loads[3]):
        copy.wait()
    named = lax.broadcasted_iota(jnp.int32, (experts, tok_dev), 0)
    first_of = (named == routes_t[0:1, :]).astype(F32)
    second_of = (named == routes_t[1:2, :]).astype(F32)
    before = (
        lax.broadcasted_iota(jnp.int32, (tok_dev, tok_dev), 0)
        < lax.broadcasted_iota(jnp.int32, (tok_dev, tok_dev), 1)
    ).astype(F32).astype(BF16)
    earlier = dot((first_of + second_of).astype(BF16), before, (1, 0))
    slot_iota = lax.broadcasted_iota(jnp.int32, (experts * cap, tok_dev), 0)
    gate_col = jnp.zeros((experts * cap, 1), F32)
    for k, of in ((0, first_of), (1, second_of)):
        rank = jnp.sum(earlier * of, axis=0, keepdims=True).astype(jnp.int32)
        taken = (slot_iota == routes_t[k : k + 1, :] * cap + rank).astype(F32)
        place[k] = taken.astype(BF16)
        gate_col = gate_col + jnp.sum(taken * gates_t[k : k + 1, :], axis=1, keepdims=True)
    both = place[0] + place[1]
    by_slot = (zs, per_dev, cap, cols)

    a2a = [
        [
            [
                remote(
                    slots.at[a, (z + step) % zs, j], zgot.at[a, z, j],
                    a2a_s.at[a, j, step - 1], a2a_r.at[a, j, step - 1], (z + step) % zs, d,
                )
                for step in range(1, zs)
            ]
            for j in range(per_dev)
        ]
        for a in range(2)
    ]

    def exchange(a, j):
        for copy in a2a[a][j]:
            copy.start()

    def arrive(a, j):
        for copy in a2a[a][j]:
            copy.wait()

    def ag_copies(at, send, recv):
        made = []
        for i, (block, to) in enumerate(
            ((d, xn), (d, yn), (d, mate_d), (second, first), (xn, mate_d), (yn, mate_d), (dd, mate_d))
        ):
            made.append(remote(at(block), at(block), send.at[i], recv.at[i], z, to))
        return made

    ag_own = [ag_copies(lambda b, a=a: own.at[a, b], own_s.at[a], own_r.at[a]) for a in range(2)]
    ag_rest = [
        [
            ag_copies(lambda b, a=a, j=j: rest.at[a, j, b], rest_s.at[a, j], rest_r.at[a, j])
            for j in range(per_dev)
        ]
        for a in range(2)
    ]

    def own_start(a):
        own[a, pl.ds(d, 1)] = slots[a, pl.ds(z, 1), :, :, 0:head]
        for copy in ag_own[a][:3]:
            copy.start()

    def assemble(a, j):
        mine = slots[a, z, j].astype(F32)
        far = [zgot[a, (z + i) % zs, j].astype(F32) for i in range(1, zs)]
        whole = jnp.concatenate([mine[:, head:]] + far, axis=-1)
        rest[a, j, pl.ds(d, 1)] = whole.astype(BF16)[None]
        for copy in ag_rest[a][j][:3]:
            copy.start()

    def forward(copies):
        copies[0].wait_recv()
        copies[1].wait_recv()
        for i in (3, 4, 5):
            copies[i].start()

    def forward_last(copies):
        copies[3].wait_recv()
        copies[6].start()

    def landed_all(copies):
        for i in (2, 4, 5, 6):
            copies[i].wait_recv()

    chips = rows.shape[2] // (2 * cap)

    def finish(a, j, here):
        def pair(n, carry):
            half = n // (chips // 2)
            chip = (n % (chips // 2)) * 2
            blocks = []
            for b in (2 * chip + half, 2 * chip + 2 + half):
                whole = jnp.concatenate([own[a, b, j].astype(F32), rest[a, j, b].astype(F32)], axis=-1)
                if here:
                    turn = width - here * cols
                    whole = jnp.concatenate([whole[:, turn:], whole[:, :turn]], axis=-1)
                blocks.append(whole)
            at = pl.ds(pl.multiple_of(n * 2 * cap, 2 * cap), 2 * cap)
            rows[a, j, at, :] = jnp.concatenate(blocks, axis=0).astype(BF16)
            return carry

        lax.fori_loop(0, chips, pair, 0)

    def finish_x(j):
        landed_all(ag_rest[0][j])
        finish(0, j, 0)

    def finish_dy(j):
        landed_all(ag_rest[1][j])
        for here in range(zs):

            @pl.when(z == here)
            def _():
                finish(1, j, here)

    def activation(j, lo, hi):
        for start, end in tiles_of(lo, hi):
            v = dot(rows[0, j], w_in[j, :, start:end], (1, 0))
            scale = 0.7978845608028654
            sq = v * v
            t = jnp.tanh(scale * v * (1.0 + 0.044715 * sq))
            half = 0.5 * (1.0 + t)
            hid[j, :, start:end] = (v * half).astype(BF16)
            slope[j, :, start:end] = half + 0.5 * v * (1.0 - t * t) * (scale * (1.0 + 0.134145 * sq))

    def backward(j, lo, hi):
        for start, end in tiles_of(lo, hi):
            dh = dot(rows[1, j], w_out[j, start:end, :], (1, 1))
            dpre[j, :, start:end] = (slope[j, :, start:end] * dh).astype(BF16)

    def hops_of(sums, relay, land, send, recv):
        return [
            remote(src, land.at[i], send.at[i], recv.at[i], z, to)
            for i, (src, to) in enumerate(
                ((sums.at[dd // 2], first), (sums.at[first // 2], first), (relay, second))
            )
        ]

    swaps = [
        [
            remote(term.at[a, j, 1 - core], mate.at[a, j], mates_s.at[a, j], mates_r.at[a, j], z, mate_d)
            for j in range(per_dev)
        ]
        for a in range(2)
    ]
    hops_r = [
        [
            hops_of(sums_r.at[a, j], relay_r.at[a, j], land_r.at[a, j], rs_s.at[a, j], rs_r.at[a, j])
            for j in range(per_dev)
        ]
        for a in range(2)
    ]
    hops_w = [
        hops_of(sums_w.at[a], relay_w.at[a], land_w.at[a], rsw_s.at[a], rsw_r.at[a]) for a in range(2)
    ]

    def terms(a, j, lo, hi):
        for start, end in tiles_of(lo, hi):
            if a == 0:
                v = dot(hid[j], w_out[j, :, start:end], (1, 0))
            else:
                v = dot(dpre[j], w_in[j, start:end, :], (1, 1))
            term[a, j, :, :, :, start:end] = v.reshape(2, chips, cap, end - start).astype(BF16)

    def swap(a, j):
        swaps[a][j].start()

    def split_sums(a, j, here):
        def chip(c, carry):
            total = term[a, j, core, c].astype(F32) + mate[a, j, c].astype(F32)
            if here:
                turn = here * cols
                total = jnp.concatenate([total[:, turn:], total[:, :turn]], axis=-1)
            sums_r[a, j, c] = total[:, head:].astype(BF16)
            sums_w[a, c, j] = total[:, :head].astype(BF16)
            return carry

        lax.fori_loop(0, chips, chip, 0)

    def sums(a, j):
        swaps[a][j].wait()
        if a == 1:
            split_sums(1, j, 0)
        else:
            for here in range(zs):

                @pl.when(z == here)
                def _():
                    split_sums(0, j, here)

        hops_r[a][j][0].start()
        hops_r[a][j][1].start()

    def own_hops(a):
        hops_w[a][0].start()
        hops_w[a][1].start()

    def pass_on(a, j):
        hops_r[a][j][0].wait()
        relay_r[a, j] = (sums_r[a, j, second // 2].astype(F32) + land_r[a, j, 0].astype(F32)).astype(BF16)
        hops_r[a][j][2].start()

    def own_pass(a):
        hops_w[a][0].wait()
        relay_w[a] = (sums_w[a, second // 2].astype(F32) + land_w[a, 0].astype(F32)).astype(BF16)
        hops_w[a][2].start()

    back = [
        [
            [
                remote(
                    zsend.at[a, step - 1, j], zback.at[a, z, j],
                    back_s.at[a, j, step - 1], back_r.at[a, j, step - 1], (z + step) % zs, d,
                )
                for step in range(1, zs)
            ]
            for j in range(per_dev)
        ]
        for a in range(2)
    ]

    def end(a, j):
        hops_r[a][j][1].wait()
        hops_r[a][j][2].wait()
        total = (
            sums_r[a, j, d // 2].astype(F32) + land_r[a, j, 1].astype(F32) + land_r[a, j, 2].astype(F32)
        )
        tail = cols - head
        for i in range(zs - 1):
            zsend[a, i, j] = total[:, tail + i * cols : tail + (i + 1) * cols].astype(BF16)
        for copy in back[a][j]:
            copy.start()
        tails[a, j] = total[:, :tail]

    def own_end(a):
        hops_w[a][1].wait()
        hops_w[a][2].wait()
        total = sums_w[a, d // 2].astype(F32) + land_w[a, 1].astype(F32) + land_w[a, 2].astype(F32)
        zback[a, pl.ds(z, 1)] = jnp.concatenate([total, tails[a]], axis=-1).astype(BF16)[None]

    def weight_grad_out(j, lo, hi):
        for start, end in tiles_of(lo, hi):
            go[j, start:end, :] = dot(hid[j, :, start:end], rows[1, j], (0, 0)).astype(BF16)

    def weight_grad_in(j, lo, hi):
        for start, end in tiles_of(lo, hi):
            gi[j, start:end, :] = dot(rows[0, j, :, start:end], dpre[j], (0, 0)).astype(BF16)

    gg = []
    for step in range(1, zs):
        gg.append(
            remote(
                gpart.at[z], gpart.at[z], gg_s.at[step - 1], gg_r.at[step - 1], (z + step) % zs, d
            )
        )

    def views_of(a):
        slot_rows = zback[a].astype(F32).reshape(experts * cap, cols).astype(BF16)
        return [dot(slot_rows, place[k], (0, 0)) for k in range(2)]

    def combine_out():
        for j in range(per_dev):
            for copy in back[0][j]:
                copy.wait()
        views = views_of(0)
        out_ref[...] = (views[0] * gates_t[0:1, :] + views[1] * gates_t[1:2, :]).astype(BF16)
        cot = cot_ref[...].astype(F32)
        inner = [jnp.sum(cot * v, axis=0, keepdims=True) for v in views]
        row = lax.broadcasted_iota(jnp.int32, (8, tok_dev), 0)
        gpart[pl.ds(z, 1)] = jnp.where(row == 0, inner[0], inner[1])[None]
        for copy in gg:
            copy.start()

    def combine_tok():
        for j in range(per_dev):
            for copy in back[1][j]:
                copy.wait()
        views = views_of(1)
        gtok_ref[...] = (views[0] + views[1]).astype(BF16)

    def weights_in():
        for copy in w_copies:
            copy.wait()

    def grad_gates():
        for copy in gg:
            copy.wait()
        total = gpart[0] + gpart[1] + gpart[2] + gpart[3]
        gg_ref[...] = total[0:2]

    slots[0] = dot(both, tok_ref[...], (1, 1)).reshape(by_slot).astype(BF16)
    pl.semaphore_wait(barrier, zs + 2)
    exchange(0, 0)
    own_start(0)
    exchange(0, 1)
    slots[1] = (dot(both, cot_ref[...], (1, 1)) * gate_col).reshape(by_slot).astype(BF16)
    own_start(1)
    forward(ag_own[0])
    arrive(0, 0)
    assemble(0, 0)
    exchange(1, 0)
    forward(ag_own[1])
    forward_last(ag_own[0])
    arrive(0, 1)
    assemble(0, 1)
    exchange(1, 1)
    forward_last(ag_own[1])
    forward(ag_rest[0][0])
    arrive(1, 0)
    assemble(1, 0)
    forward(ag_rest[0][1])
    forward_last(ag_rest[0][0])
    weights_in()
    landed_all(ag_own[0])
    finish_x(0)
    activation(0, 0, 256)
    arrive(1, 1)
    assemble(1, 1)
    activation(0, 256, hidden_here)
    forward_last(ag_rest[0][1])
    forward(ag_rest[1][0])
    terms(0, 0, 0, width)
    swap(0, 0)
    finish_x(1)
    activation(1, 0, 512)
    forward(ag_rest[1][1])
    forward_last(ag_rest[1][0])
    sums(0, 0)
    activation(1, 512, hidden_here)
    terms(0, 1, 0, width)
    swap(0, 1)
    forward_last(ag_rest[1][1])
    landed_all(ag_own[1])
    finish_dy(0)
    backward(0, 0, hidden_here)
    sums(0, 1)
    own_hops(0)
    pass_on(0, 0)
    terms(1, 0, 0, width)
    swap(1, 0)
    finish_dy(1)
    backward(1, 0, hidden_here)
    sums(1, 0)
    terms(1, 1, 0, width)
    swap(1, 1)
    pass_on(0, 1)
    own_pass(0)
    end(0, 0)
    weight_grad_out(0, 0, 512)
    sums(1, 1)
    end(0, 1)
    own_end(0)
    weight_grad_out(0, 512, hidden_here)
    pass_on(1, 0)
    weight_grad_out(1, 0, 512)
    pass_on(1, 1)
    own_hops(1)
    weight_grad_out(1, 512, hidden_here)
    end(1, 0)
    own_pass(1)
    combine_out()
    end(1, 1)
    weight_grad_in(0, 0, width)
    weight_grad_in(1, 0, width)
    own_end(1)
    grad_gates()
    combine_tok()
    for a in range(2):
        for copy in ag_own[a]:
            copy.wait_send()
        for j in range(per_dev):
            for copy in ag_rest[a][j]:
                copy.wait_send()


def store_kernel(out_in, gtok_in, gg_in, gi, go, out_hbm, gtok_hbm, gg_hbm, gi_hbm, go_hbm, sem, wsem):
    per_dev, width, _ = gi.shape
    zs = wsem.shape[1] - 1
    cols = width // zs
    z = lax.axis_index("expert")
    copies = []
    for j in range(per_dev):
        copies.append(pltpu.make_async_copy(go.at[j], go_hbm.at[j], wsem.at[j, zs]))
        for i in range(zs):
            piece = pl.ds(pl.multiple_of(((z + i) % zs) * cols, 16), cols)
            copies.append(
                pltpu.make_async_copy(gi.at[j, i * cols : (i + 1) * cols], gi_hbm.at[j, piece], wsem.at[j, i])
            )
    for i, (here, there) in enumerate(((out_in, out_hbm), (gtok_in, gtok_hbm), (gg_in, gg_hbm))):
        copies.append(pltpu.make_async_copy(here, there, sem.at[i]))
    for copy in copies:
        copy.start()
    for copy in copies:
        copy.wait()


def fused_shards(tokens, routes, gate_values, expert_in, expert_out, cotangent):
    tok_dev, cols = tokens.shape
    zs = lax.axis_size("expert")
    dps = lax.axis_size("dp")
    per_dev, width, hidden_here = expert_in.shape
    experts = per_dev * zs
    cap = 5 * tok_dev // (2 * experts)
    all_rows = dps * cap
    head = cols // 128 * 128
    others = width - head
    chips = dps // 2
    vmem = pl.BlockSpec(memory_space=pltpu.VMEM)
    hbm = pl.BlockSpec(memory_space=pl.ANY)
    dma = pltpu.SemaphoreType.DMA

    results = pl.pallas_call(
        layer_kernel,
        out_shape=(
            pltpu.VMEM((cols, tok_dev), BF16),
            pltpu.VMEM((cols, tok_dev), BF16),
            pltpu.VMEM((2, tok_dev), F32),
            pltpu.VMEM(expert_in.shape, BF16),
            pltpu.VMEM(expert_out.shape, BF16),
        ),
        in_specs=[hbm] * 6,
        out_specs=(vmem,) * 5,
        scratch_shapes=[
            pltpu.VMEM((cols, tok_dev), BF16),
            pltpu.VMEM((cols, tok_dev), BF16),
            pltpu.VMEM((2, tok_dev), jnp.int32),
            pltpu.VMEM((2, tok_dev), F32),
            pltpu.VMEM(expert_in.shape, BF16),
            pltpu.VMEM(expert_out.shape, BF16),
            pltpu.VMEM((2, zs, per_dev, cap, cols), BF16),
            pltpu.VMEM((2, zs, per_dev, cap, cols), BF16),
            pltpu.VMEM((2, dps, per_dev, cap, head), BF16),
            pltpu.VMEM((2, per_dev, dps, cap, others), BF16),
            pltpu.VMEM((2, per_dev, all_rows, width), BF16),
            pltpu.VMEM((per_dev, all_rows, hidden_here), BF16),
            pltpu.VMEM((per_dev, all_rows, hidden_here), F32),
            pltpu.VMEM((per_dev, all_rows, hidden_here), BF16),
            pltpu.VMEM((2, per_dev, 2, chips, cap, width), BF16),
            pltpu.VMEM((2, per_dev, chips, cap, width), BF16),
            pltpu.VMEM((2, per_dev, chips, cap, others), BF16),
            pltpu.VMEM((2, per_dev, cap, others), BF16),
            pltpu.VMEM((2, per_dev, 3, cap, others), BF16),
            pltpu.VMEM((2, chips, per_dev, cap, head), BF16),
            pltpu.VMEM((2, per_dev, cap, head), BF16),
            pltpu.VMEM((2, 3, per_dev, cap, head), BF16),
            pltpu.VMEM((2, per_dev, cap, cols - head), F32),
            pltpu.VMEM((2, zs - 1, per_dev, cap, cols), BF16),
            pltpu.VMEM((2, zs, per_dev, cap, cols), BF16),
            pltpu.VMEM((2, experts * cap, tok_dev), BF16),
            pltpu.VMEM((zs, 8, tok_dev), F32),
            dma((4,)),
            dma((per_dev, zs + 1)),
            dma((2, per_dev, zs - 1)), dma((2, per_dev, zs - 1)),
            dma((2, 7)), dma((2, 7)),
            dma((2, per_dev, 7)), dma((2, per_dev, 7)),
            dma((2, per_dev)), dma((2, per_dev)),
            dma((2, per_dev, 3)), dma((2, per_dev, 3)),
            dma((2, 3)), dma((2, 3)),
            dma((2, per_dev, zs - 1)), dma((2, per_dev, zs - 1)),
            dma((zs - 1,)), dma((zs - 1,)),
        ],
        compiler_params=pltpu.CompilerParams(
            collective_id=0, has_side_effects=True, vmem_limit_bytes=48 * 1024 * 1024
        ),
    )(tokens.T, cotangent.T, routes.T, gate_values.T, expert_in, expert_out)
    layer_t, gtok_t, gates_grad_t, grad_in, grad_out = pl.pallas_call(
        store_kernel,
        out_shape=(
            jax.ShapeDtypeStruct((cols, tok_dev), BF16),
            jax.ShapeDtypeStruct((cols, tok_dev), BF16),
            jax.ShapeDtypeStruct((2, tok_dev), F32),
            jax.ShapeDtypeStruct(expert_in.shape, BF16),
            jax.ShapeDtypeStruct(expert_out.shape, BF16),
        ),
        in_specs=[vmem] * 5,
        out_specs=(hbm,) * 5,
        scratch_shapes=[dma((3,)), dma((per_dev, zs + 1))],
        compiler_params=pltpu.CompilerParams(vmem_limit_bytes=1024 * 1024),
    )(*results)
    return (layer_t.T, gtok_t.T, gates_grad_t.T, grad_in, grad_out)


def solution(mesh):
    placed = (
        P("dp", "expert"),
        P("dp", None),
        P("dp", None),
        P("expert", None, "dp"),
        P("expert", "dp", None),
        P("dp", "expert"),
    )
    fused = mesh.shape["expert"] == 4 and mesh.shape["dp"] == 8
    return jax.shard_map(
        fused_shards if fused else shards,
        mesh=mesh,
        in_specs=placed,
        out_specs=(
            P("dp", "expert"),
            P("dp", "expert"),
            P("dp", None),
            P("expert", None, "dp"),
            P("expert", "dp", None),
        ),
        check_vma=False,
    )
```

```python
import jax
import jax.numpy as jnp
from jax import lax
from jax.experimental import pallas as pl
from jax.experimental.pallas import tpu as pltpu
from jax.sharding import PartitionSpec as P


def gelu_tanh(values):
    return jax.nn.gelu(values, approximate=True)


def shards(tokens, routes, gate_values, expert_in, expert_out, cotangent):
    tok_dev, columns = tokens.shape
    groups = lax.axis_size("expert")
    per_dev = expert_in.shape[0]
    experts = per_dev * groups
    capacity = 5 * tok_dev // (2 * experts)
    full_width = columns * groups
    slot_rows = per_dev * capacity
    slot_count = experts * capacity
    flat_routes = routes.reshape(-1)
    pairs_here = flat_routes.shape[0]
    places = jnp.arange(pairs_here, dtype=jnp.int32)
    same = flat_routes[:, None] == flat_routes[None, :]
    rank_in = jnp.sum((same & (places[None, :] < places[:, None])).astype(jnp.int32), axis=1)
    owner_idx = flat_routes // per_dev
    within = flat_routes % per_dev
    slot_ids = (within * capacity + rank_in) * groups + owner_idx
    placing = (slot_ids[:, None] == jnp.arange(slot_count, dtype=jnp.int32)[None, :]).astype(
        jnp.bfloat16
    )
    pair_gates = gate_values.reshape(-1)
    pair_tokens = jnp.repeat(tokens, 2, axis=0)
    cot_float = cotangent.astype(jnp.float32)
    pair_cot = (jnp.repeat(cot_float, 2, axis=0) * pair_gates[:, None]).astype(jnp.bfloat16)

    def to_slots(pairs):
        slots = jnp.einsum("ps,pc->sc", placing, pairs, preferred_element_type=jnp.float32)
        return slots.astype(jnp.bfloat16).reshape(slot_rows, groups, columns)

    def from_slots(back):
        return jnp.einsum(
            "ps,sc->pc",
            placing,
            back.reshape(slot_count, columns),
            preferred_element_type=jnp.float32,
        )

    def as_rows(gathered):
        return gathered.reshape(-1, per_dev, capacity, full_width)

    x_moved = lax.all_to_all(
        to_slots(pair_tokens), "expert", split_axis=1, concat_axis=1, tiled=True
    )
    x_rows = as_rows(
        lax.all_gather(x_moved.reshape(slot_rows, full_width), "dp", axis=0, tiled=True)
    )
    pre_act = jnp.einsum("bjcd,jdf->bjcf", x_rows, expert_in, preferred_element_type=jnp.float32)
    pre_act, hidden = (pre_act, gelu_tanh(pre_act).astype(jnp.bfloat16))
    part = hidden
    term = jnp.einsum("bjcf,jfd->bjcd", part, expert_out, preferred_element_type=jnp.float32)
    out_sum = lax.psum_scatter(
        term.reshape(lax.axis_size("dp") * slot_rows, full_width).astype(jnp.bfloat16),
        "dp",
        scatter_dimension=0,
        tiled=True,
    )
    out_back = lax.all_to_all(
        out_sum.reshape(slot_rows, groups, columns),
        "expert",
        split_axis=1,
        concat_axis=1,
        tiled=True,
    )
    dy_moved = lax.all_to_all(to_slots(pair_cot), "expert", split_axis=1, concat_axis=1, tiled=True)
    dy_rows = as_rows(
        lax.all_gather(dy_moved.reshape(slot_rows, full_width), "dp", axis=0, tiled=True)
    )
    d_hidden = jnp.einsum("bjcd,jfd->bjcf", dy_rows, expert_out, preferred_element_type=jnp.float32)
    backward_d_pre = jax.vjp(gelu_tanh, pre_act)[1](d_hidden)[0].astype(jnp.bfloat16)
    grad_out = jnp.einsum("bjcf,bjcd->jfd", hidden, dy_rows, preferred_element_type=jnp.float32)
    grad_in = jnp.einsum(
        "bjcd,bjcf->jdf", x_rows, backward_d_pre, preferred_element_type=jnp.float32
    )
    d_pre, grad_in, grad_out = (
        backward_d_pre,
        grad_in.astype(jnp.bfloat16),
        grad_out.astype(jnp.bfloat16),
    )
    part = d_pre
    term = jnp.einsum("bjcf,jdf->bjcd", part, expert_in, preferred_element_type=jnp.float32)
    dx_sum = lax.psum_scatter(
        term.reshape(lax.axis_size("dp") * slot_rows, full_width).astype(jnp.bfloat16),
        "dp",
        scatter_dimension=0,
        tiled=True,
    )
    dx_back = lax.all_to_all(
        dx_sum.reshape(slot_rows, groups, columns),
        "expert",
        split_axis=1,
        concat_axis=1,
        tiled=True,
    )
    out_view = from_slots(out_back).reshape(tok_dev, 2, columns)
    dx_view = from_slots(dx_back).reshape(tok_dev, 2, columns)
    gate_pairs = pair_gates.reshape(tok_dev, 2)
    layer_out = (out_view[:, 0] * gate_pairs[:, 0:1] + out_view[:, 1] * gate_pairs[:, 1:2]).astype(
        jnp.bfloat16
    )
    grad_tokens = (dx_view[:, 0] + dx_view[:, 1]).astype(jnp.bfloat16)
    gate_part = jnp.sum(cot_float[:, None, :] * out_view, axis=2)
    grad_gates = lax.psum(gate_part, "expert")
    return (layer_out, grad_tokens, grad_gates, grad_in, grad_out)


MESH = pl.DeviceIdType.MESH
BF16 = jnp.bfloat16
F32 = jnp.float32


def tiles_of(lo, hi, step=256):
    return [(at, min(at + step, hi)) for at in range(lo, hi, step)]


def dot(left, right, contract):
    return lax.dot_general(left, right, ((contract[:1], contract[1:]), ((), ())), preferred_element_type=F32)


def layer_kernel(
    tok_hbm, cot_hbm, routes_hbm, gates_hbm, w_in_hbm, w_out_hbm,
    out_ref, gtok_ref, gg_ref, gi, go,
    tok_ref, cot_ref, routes_t, gates_t,
    w_in, w_out, slots, zgot, own, rest, rows, hid, slope, dpre,
    term, mate, sums_r, relay_r, land_r, sums_w, relay_w, land_w, totals, zsend, zback, place, gpart,
    isem, wsem, a2a_s, a2a_r, own_s, own_r, rest_s, rest_r, mates_s, mates_r, rs_s, rs_r, rsw_s, rsw_r,
    back_s, back_r, gg_s, gg_r,
):
    cols, tok_dev = tok_ref.shape
    zs, per_dev, cap = slots.shape[1:4]
    width, hidden_here = w_in.shape[1:]
    head = own.shape[-1]
    experts = zs * per_dev
    z = lax.axis_index("expert")
    d = lax.axis_index("dp")
    core = d % 2
    xbit = (d // 2) % 2
    ybit = d // 4
    mate_d = d + 1 - 2 * core
    xn = d + 2 - 4 * xbit
    yn = d + 4 - 8 * ybit
    dd = xn + 4 - 8 * ybit
    first = core * yn + (1 - core) * xn
    second = core * xn + (1 - core) * yn

    def remote(src, dst, send, recv, zi, di):
        return pltpu.make_async_remote_copy(
            src_ref=src, dst_ref=dst, send_sem=send, recv_sem=recv, device_id=(zi, di), device_id_type=MESH
        )

    loads = [
        pltpu.make_async_copy(src, dst, isem.at[i])
        for i, (src, dst) in enumerate(
            ((routes_hbm, routes_t), (tok_hbm, tok_ref), (gates_hbm, gates_t), (cot_hbm, cot_ref))
        )
    ]
    for copy in loads:
        copy.start()
    barrier = pltpu.get_barrier_semaphore()
    for step in range(1, zs):
        pl.semaphore_signal(barrier, inc=1, device_id=((z + step) % zs, d), device_id_type=MESH)
    for other in (mate_d, xn, yn):
        pl.semaphore_signal(barrier, inc=1, device_id=(z, other), device_id_type=MESH)

    w_copies = []
    for j in range(per_dev):
        for i in range(zs):
            piece = pl.ds(pl.multiple_of(((z + i) % zs) * cols, 16), cols)
            w_copies.append(
                pltpu.make_async_copy(
                    w_in_hbm.at[j, piece], w_in.at[j, i * cols : (i + 1) * cols], wsem.at[j, i]
                )
            )
    for j in range(per_dev):
        w_copies.append(pltpu.make_async_copy(w_out_hbm.at[j], w_out.at[j], wsem.at[j, zs]))
    for copy in w_copies:
        copy.start()

    for copy in (loads[0], loads[2], loads[1], loads[3]):
        copy.wait()
    named = lax.broadcasted_iota(jnp.int32, (experts, tok_dev), 0)
    first_of = (named == routes_t[0:1, :]).astype(F32)
    second_of = (named == routes_t[1:2, :]).astype(F32)
    before = (
        lax.broadcasted_iota(jnp.int32, (tok_dev, tok_dev), 0)
        < lax.broadcasted_iota(jnp.int32, (tok_dev, tok_dev), 1)
    ).astype(F32).astype(BF16)
    earlier = dot((first_of + second_of).astype(BF16), before, (1, 0))
    slot_iota = lax.broadcasted_iota(jnp.int32, (experts * cap, tok_dev), 0)
    gate_col = jnp.zeros((experts * cap, 1), F32)
    for k, of in ((0, first_of), (1, second_of)):
        rank = jnp.sum(earlier * of, axis=0, keepdims=True).astype(jnp.int32)
        taken = (slot_iota == routes_t[k : k + 1, :] * cap + rank).astype(F32)
        place[k] = taken.astype(BF16)
        gate_col = gate_col + jnp.sum(taken * gates_t[k : k + 1, :], axis=1, keepdims=True)
    both = place[0] + place[1]
    by_slot = (zs, per_dev, cap, cols)

    a2a = [
        [
            [
                remote(
                    slots.at[a, (z + step) % zs, j], zgot.at[a, z, j],
                    a2a_s.at[a, j, step - 1], a2a_r.at[a, j, step - 1], (z + step) % zs, d,
                )
                for step in range(1, zs)
            ]
            for j in range(per_dev)
        ]
        for a in range(2)
    ]

    def exchange(a, j):
        for copy in a2a[a][j]:
            copy.start()

    def arrive(a, j):
        for copy in a2a[a][j]:
            copy.wait()

    def ag_copies(at, send, recv):
        made = []
        for i, (block, to) in enumerate(
            ((d, xn), (d, yn), (d, mate_d), (second, first), (xn, mate_d), (yn, mate_d), (dd, mate_d))
        ):
            made.append(remote(at(block), at(block), send.at[i], recv.at[i], z, to))
        return made

    ag_own = [ag_copies(lambda b, a=a: own.at[a, b], own_s.at[a], own_r.at[a]) for a in range(2)]
    ag_rest = [
        [
            ag_copies(lambda b, a=a, j=j: rest.at[a, j, b], rest_s.at[a, j], rest_r.at[a, j])
            for j in range(per_dev)
        ]
        for a in range(2)
    ]

    def own_start(a):
        own[a, pl.ds(d, 1)] = slots[a, pl.ds(z, 1), :, :, 0:head]
        for copy in ag_own[a][:3]:
            copy.start()

    def assemble(a, j):
        mine = slots[a, z, j].astype(F32)
        far = [zgot[a, (z + i) % zs, j].astype(F32) for i in range(1, zs)]
        whole = jnp.concatenate([mine[:, head:]] + far, axis=-1)
        rest[a, j, pl.ds(d, 1)] = whole.astype(BF16)[None]
        for copy in ag_rest[a][j][:3]:
            copy.start()

    def forward(copies):
        copies[0].wait_recv()
        copies[1].wait_recv()
        for i in (3, 4, 5):
            copies[i].start()

    def forward_last(copies):
        copies[3].wait_recv()
        copies[6].start()

    def landed_all(copies):
        for i in (2, 4, 5, 6):
            copies[i].wait_recv()

    chips = rows.shape[2] // (2 * cap)

    def finish(a, j, here):
        def pair(n, carry):
            half = n // (chips // 2)
            chip = (n % (chips // 2)) * 2
            blocks = []
            for b in (2 * chip + half, 2 * chip + 2 + half):
                whole = jnp.concatenate([own[a, b, j].astype(F32), rest[a, j, b].astype(F32)], axis=-1)
                if here:
                    turn = width - here * cols
                    whole = jnp.concatenate([whole[:, turn:], whole[:, :turn]], axis=-1)
                blocks.append(whole)
            at = pl.ds(pl.multiple_of(n * 2 * cap, 2 * cap), 2 * cap)
            rows[a, j, at, :] = jnp.concatenate(blocks, axis=0).astype(BF16)
            return carry

        lax.fori_loop(0, chips, pair, 0)

    def finish_x(j):
        landed_all(ag_rest[0][j])
        finish(0, j, 0)

    def finish_dy(j):
        landed_all(ag_rest[1][j])
        for here in range(zs):

            @pl.when(z == here)
            def _():
                finish(1, j, here)

    def activation(j, lo, hi):
        for start, end in tiles_of(lo, hi):
            v = dot(rows[0, j], w_in[j, :, start:end], (1, 0))
            scale = 0.7978845608028654
            sq = v * v
            t = jnp.tanh(scale * v * (1.0 + 0.044715 * sq))
            half = 0.5 * (1.0 + t)
            hid[j, :, start:end] = (v * half).astype(BF16)
            slope[j, :, start:end] = half + 0.5 * v * (1.0 - t * t) * (scale * (1.0 + 0.134145 * sq))

    def backward(j, lo, hi):
        for start, end in tiles_of(lo, hi):
            dh = dot(rows[1, j], w_out[j, start:end, :], (1, 1))
            dpre[j, :, start:end] = (slope[j, :, start:end] * dh).astype(BF16)

    def hops_of(sums, relay, land, send, recv):
        return [
            remote(src, land.at[i], send.at[i], recv.at[i], z, to)
            for i, (src, to) in enumerate(
                ((sums.at[dd // 2], first), (sums.at[first // 2], first), (relay, second))
            )
        ]

    swaps = [
        [
            remote(term.at[a, j, 1 - core], mate.at[a, j], mates_s.at[a, j], mates_r.at[a, j], z, mate_d)
            for j in range(per_dev)
        ]
        for a in range(2)
    ]
    others = sums_r.shape[-1]
    cut = 512
    spans = [[[(0, cut), (cut, others)] for j in range(per_dev)] for a in range(2)]

    def hops_at(a, j, k):
        lo, hi = spans[a][j][k]
        return hops_of(
            sums_r.at[a, j, :, :, lo:hi], relay_r.at[a, j, :, lo:hi], land_r.at[a, j, :, :, lo:hi],
            rs_s.at[a, j, k], rs_r.at[a, j, k],
        )

    hops_r = [[[hops_at(a, j, k) for k in range(len(spans[a][j]))] for j in range(per_dev)] for a in range(2)]
    hops_w = [
        hops_of(sums_w.at[a], relay_w.at[a], land_w.at[a], rsw_s.at[a], rsw_r.at[a]) for a in range(2)
    ]

    def terms(a, j, lo, hi):
        for start, end in tiles_of(lo, hi):
            if a == 0:
                v = dot(hid[j], w_out[j, :, start:end], (1, 0))
            else:
                v = dot(dpre[j], w_in[j, start:end, :], (1, 1))
            term[a, j, :, :, :, start:end] = v.reshape(2, chips, cap, end - start).astype(BF16)

    def swap(a, j):
        swaps[a][j].start()

    def split_sums(a, j, here):
        def chip(c, carry):
            total = term[a, j, core, c].astype(F32) + mate[a, j, c].astype(F32)
            if here:
                turn = here * cols
                total = jnp.concatenate([total[:, turn:], total[:, :turn]], axis=-1)
            sums_r[a, j, c] = total[:, head:].astype(BF16)
            sums_w[a, c, j] = total[:, :head].astype(BF16)
            return carry

        lax.fori_loop(0, chips, chip, 0)

    def sums(a, j):
        swaps[a][j].wait()
        if a == 1:
            split_sums(1, j, 0)
        else:
            for here in range(zs):

                @pl.when(z == here)
                def _():
                    split_sums(0, j, here)

        for hops in hops_r[a][j]:
            hops[0].start()
            hops[1].start()

    def own_hops(a):
        hops_w[a][0].start()
        hops_w[a][1].start()

    def pass_on(a, j, k):
        lo, hi = spans[a][j][k]
        hops_r[a][j][k][0].wait()
        both_ways = sums_r[a, j, second // 2, :, lo:hi].astype(F32) + land_r[a, j, 0, :, lo:hi].astype(F32)
        relay_r[a, j, :, lo:hi] = both_ways.astype(BF16)
        hops_r[a][j][k][2].start()

    def own_pass(a):
        hops_w[a][0].wait()
        relay_w[a] = (sums_w[a, second // 2].astype(F32) + land_w[a, 0].astype(F32)).astype(BF16)
        hops_w[a][2].start()

    back = [
        [
            [
                remote(
                    zsend.at[a, step - 1, j], zback.at[a, z, j],
                    back_s.at[a, j, step - 1], back_r.at[a, j, step - 1], (z + step) % zs, d,
                )
                for step in range(1, zs)
            ]
            for j in range(per_dev)
        ]
        for a in range(2)
    ]

    def end(a, j, k):
        lo, hi = spans[a][j][k]
        hops_r[a][j][k][1].wait()
        hops_r[a][j][k][2].wait()
        here = sums_r[a, j, d // 2, :, lo:hi].astype(F32)
        totals[a, j, :, lo:hi] = here + land_r[a, j, 1, :, lo:hi].astype(F32) + land_r[a, j, 2, :, lo:hi].astype(F32)
        tail = cols - head
        for i in range(zs - 1):
            start = tail + i * cols
            if lo < start + cols <= hi:
                zsend[a, i, j] = totals[a, j, :, start : start + cols].astype(BF16)
                back[a][j][i].start()

    def own_end(a):
        hops_w[a][1].wait()
        hops_w[a][2].wait()
        total = sums_w[a, d // 2].astype(F32) + land_w[a, 1].astype(F32) + land_w[a, 2].astype(F32)
        zback[a, pl.ds(z, 1)] = jnp.concatenate([total, totals[a, :, :, 0 : cols - head]], axis=-1).astype(BF16)[None]

    def weight_grad_out(j, lo, hi):
        for start, end in tiles_of(lo, hi):
            go[j, start:end, :] = dot(hid[j, :, start:end], rows[1, j], (0, 0)).astype(BF16)

    def weight_grad_in(j, lo, hi):
        for start, end in tiles_of(lo, hi):
            gi[j, start:end, :] = dot(rows[0, j, :, start:end], dpre[j], (0, 0)).astype(BF16)

    gg = []
    for step in range(1, zs):
        gg.append(
            remote(
                gpart.at[z], gpart.at[z], gg_s.at[step - 1], gg_r.at[step - 1], (z + step) % zs, d
            )
        )

    def views_of(a):
        slot_rows = zback[a].astype(F32).reshape(experts * cap, cols).astype(BF16)
        return [dot(slot_rows, place[k], (0, 0)) for k in range(2)]

    def combine_out():
        for j in range(per_dev):
            for copy in back[0][j]:
                copy.wait()
        views = views_of(0)
        out_ref[...] = (views[0] * gates_t[0:1, :] + views[1] * gates_t[1:2, :]).astype(BF16)
        cot = cot_ref[...].astype(F32)
        inner = [jnp.sum(cot * v, axis=0, keepdims=True) for v in views]
        row = lax.broadcasted_iota(jnp.int32, (8, tok_dev), 0)
        gpart[pl.ds(z, 1)] = jnp.where(row == 0, inner[0], inner[1])[None]
        for copy in gg:
            copy.start()

    def combine_tok():
        for j in range(per_dev):
            for copy in back[1][j]:
                copy.wait()
        views = views_of(1)
        gtok_ref[...] = (views[0] + views[1]).astype(BF16)

    def weights_in():
        for copy in w_copies:
            copy.wait()

    def grad_gates():
        for copy in gg:
            copy.wait()
        total = gpart[0] + gpart[1] + gpart[2] + gpart[3]
        gg_ref[...] = total[0:2]

    def place_dy():
        slots[1] = (dot(both, cot_ref[...], (1, 1)) * gate_col).reshape(by_slot).astype(BF16)

    slots[0] = dot(both, tok_ref[...], (1, 1)).reshape(by_slot).astype(BF16)
    pl.semaphore_wait(barrier, zs + 2)
    exchange(0, 0)
    own_start(0)
    exchange(0, 1)
    place_dy()
    own_start(1)
    forward(ag_own[0])
    arrive(0, 0)
    assemble(0, 0)
    exchange(1, 0)
    forward(ag_own[1])
    forward_last(ag_own[0])
    arrive(0, 1)
    assemble(0, 1)
    exchange(1, 1)
    forward_last(ag_own[1])
    forward(ag_rest[0][0])
    arrive(1, 0)
    assemble(1, 0)
    forward(ag_rest[0][1])
    forward_last(ag_rest[0][0])
    weights_in()
    landed_all(ag_own[0])
    finish_x(0)
    activation(0, 0, 256)
    arrive(1, 1)
    assemble(1, 1)
    activation(0, 256, hidden_here)
    forward_last(ag_rest[0][1])
    forward(ag_rest[1][0])
    terms(0, 0, 0, width)
    swap(0, 0)
    finish_x(1)
    activation(1, 0, 512)
    forward(ag_rest[1][1])
    forward_last(ag_rest[1][0])
    sums(0, 0)
    activation(1, 512, hidden_here)
    terms(0, 1, 0, width)
    swap(0, 1)
    forward_last(ag_rest[1][1])
    landed_all(ag_own[1])
    finish_dy(0)
    backward(0, 0, hidden_here)
    sums(0, 1)
    own_hops(0)
    pass_on(0, 0, 0)
    pass_on(0, 0, 1)
    terms(1, 0, 0, width)
    swap(1, 0)
    finish_dy(1)
    backward(1, 0, hidden_here)
    sums(1, 0)
    terms(1, 1, 0, width)
    swap(1, 1)
    pass_on(0, 1, 0)
    pass_on(0, 1, 1)
    own_pass(0)
    end(0, 0, 0)
    end(0, 0, 1)
    weight_grad_out(0, 0, 512)
    sums(1, 1)
    end(0, 1, 0)
    end(0, 1, 1)
    own_end(0)
    weight_grad_out(0, 512, hidden_here)
    pass_on(1, 0, 0)
    pass_on(1, 0, 1)
    weight_grad_out(1, 0, 512)
    pass_on(1, 1, 0)
    pass_on(1, 1, 1)
    own_hops(1)
    weight_grad_out(1, 512, hidden_here)
    end(1, 0, 0)
    end(1, 0, 1)
    own_pass(1)
    combine_out()
    end(1, 1, 0)
    end(1, 1, 1)
    weight_grad_in(0, 0, width)
    weight_grad_in(1, 0, width)
    own_end(1)
    grad_gates()
    combine_tok()
    for a in range(2):
        for copy in ag_own[a]:
            copy.wait_send()
        for j in range(per_dev):
            for copy in ag_rest[a][j]:
                copy.wait_send()


def store_kernel(out_in, gtok_in, gg_in, gi, go, out_hbm, gtok_hbm, gg_hbm, gi_hbm, go_hbm, sem, wsem):
    per_dev, width, _ = gi.shape
    zs = wsem.shape[1] - 1
    cols = width // zs
    z = lax.axis_index("expert")
    copies = []
    for j in range(per_dev):
        copies.append(pltpu.make_async_copy(go.at[j], go_hbm.at[j], wsem.at[j, zs]))
        for i in range(zs):
            piece = pl.ds(pl.multiple_of(((z + i) % zs) * cols, 16), cols)
            copies.append(
                pltpu.make_async_copy(gi.at[j, i * cols : (i + 1) * cols], gi_hbm.at[j, piece], wsem.at[j, i])
            )
    for i, (here, there) in enumerate(((out_in, out_hbm), (gtok_in, gtok_hbm), (gg_in, gg_hbm))):
        copies.append(pltpu.make_async_copy(here, there, sem.at[i]))
    for copy in copies:
        copy.start()
    for copy in copies:
        copy.wait()


def fused_shards(tokens, routes, gate_values, expert_in, expert_out, cotangent):
    tok_dev, cols = tokens.shape
    zs = lax.axis_size("expert")
    dps = lax.axis_size("dp")
    per_dev, width, hidden_here = expert_in.shape
    experts = per_dev * zs
    cap = 5 * tok_dev // (2 * experts)
    all_rows = dps * cap
    head = cols // 128 * 128
    others = width - head
    chips = dps // 2
    vmem = pl.BlockSpec(memory_space=pltpu.VMEM)
    hbm = pl.BlockSpec(memory_space=pl.ANY)
    dma = pltpu.SemaphoreType.DMA

    results = pl.pallas_call(
        layer_kernel,
        out_shape=(
            pltpu.VMEM((cols, tok_dev), BF16),
            pltpu.VMEM((cols, tok_dev), BF16),
            pltpu.VMEM((2, tok_dev), F32),
            pltpu.VMEM(expert_in.shape, BF16),
            pltpu.VMEM(expert_out.shape, BF16),
        ),
        in_specs=[hbm] * 6,
        out_specs=(vmem,) * 5,
        scratch_shapes=[
            pltpu.VMEM((cols, tok_dev), BF16),
            pltpu.VMEM((cols, tok_dev), BF16),
            pltpu.VMEM((2, tok_dev), jnp.int32),
            pltpu.VMEM((2, tok_dev), F32),
            pltpu.VMEM(expert_in.shape, BF16),
            pltpu.VMEM(expert_out.shape, BF16),
            pltpu.VMEM((2, zs, per_dev, cap, cols), BF16),
            pltpu.VMEM((2, zs, per_dev, cap, cols), BF16),
            pltpu.VMEM((2, dps, per_dev, cap, head), BF16),
            pltpu.VMEM((2, per_dev, dps, cap, others), BF16),
            pltpu.VMEM((2, per_dev, all_rows, width), BF16),
            pltpu.VMEM((per_dev, all_rows, hidden_here), BF16),
            pltpu.VMEM((per_dev, all_rows, hidden_here), F32),
            pltpu.VMEM((per_dev, all_rows, hidden_here), BF16),
            pltpu.VMEM((2, per_dev, 2, chips, cap, width), BF16),
            pltpu.VMEM((2, per_dev, chips, cap, width), BF16),
            pltpu.VMEM((2, per_dev, chips, cap, others), BF16),
            pltpu.VMEM((2, per_dev, cap, others), BF16),
            pltpu.VMEM((2, per_dev, 3, cap, others), BF16),
            pltpu.VMEM((2, chips, per_dev, cap, head), BF16),
            pltpu.VMEM((2, per_dev, cap, head), BF16),
            pltpu.VMEM((2, 3, per_dev, cap, head), BF16),
            pltpu.VMEM((2, per_dev, cap, others), F32),
            pltpu.VMEM((2, zs - 1, per_dev, cap, cols), BF16),
            pltpu.VMEM((2, zs, per_dev, cap, cols), BF16),
            pltpu.VMEM((2, experts * cap, tok_dev), BF16),
            pltpu.VMEM((zs, 8, tok_dev), F32),
            dma((4,)),
            dma((per_dev, zs + 1)),
            dma((2, per_dev, zs - 1)), dma((2, per_dev, zs - 1)),
            dma((2, 7)), dma((2, 7)),
            dma((2, per_dev, 7)), dma((2, per_dev, 7)),
            dma((2, per_dev)), dma((2, per_dev)),
            dma((2, per_dev, 2, 3)), dma((2, per_dev, 2, 3)),
            dma((2, 3)), dma((2, 3)),
            dma((2, per_dev, zs - 1)), dma((2, per_dev, zs - 1)),
            dma((zs - 1,)), dma((zs - 1,)),
        ],
        compiler_params=pltpu.CompilerParams(
            collective_id=0, has_side_effects=True, vmem_limit_bytes=48 * 1024 * 1024
        ),
    )(tokens.T, cotangent.T, routes.T, gate_values.T, expert_in, expert_out)
    layer_t, gtok_t, gates_grad_t, grad_in, grad_out = pl.pallas_call(
        store_kernel,
        out_shape=(
            jax.ShapeDtypeStruct((cols, tok_dev), BF16),
            jax.ShapeDtypeStruct((cols, tok_dev), BF16),
            jax.ShapeDtypeStruct((2, tok_dev), F32),
            jax.ShapeDtypeStruct(expert_in.shape, BF16),
            jax.ShapeDtypeStruct(expert_out.shape, BF16),
        ),
        in_specs=[vmem] * 5,
        out_specs=(hbm,) * 5,
        scratch_shapes=[dma((3,)), dma((per_dev, zs + 1))],
        compiler_params=pltpu.CompilerParams(vmem_limit_bytes=1024 * 1024),
    )(*results)
    return (layer_t.T, gtok_t.T, gates_grad_t.T, grad_in, grad_out)


def solution(mesh):
    placed = (
        P("dp", "expert"),
        P("dp", None),
        P("dp", None),
        P("expert", None, "dp"),
        P("expert", "dp", None),
        P("dp", "expert"),
    )
    fused = mesh.shape["expert"] == 4 and mesh.shape["dp"] == 8
    return jax.shard_map(
        fused_shards if fused else shards,
        mesh=mesh,
        in_specs=placed,
        out_specs=(
            P("dp", "expert"),
            P("dp", "expert"),
            P("dp", None),
            P("expert", None, "dp"),
            P("expert", "dp", None),
        ),
        check_vma=False,
    )
```

```python
import jax
import jax.numpy as jnp
from jax import lax
from jax.experimental import pallas as pl
from jax.experimental.pallas import tpu as pltpu
from jax.sharding import PartitionSpec as P


def gelu_tanh(values):
    return jax.nn.gelu(values, approximate=True)


def shards(tokens, routes, gate_values, expert_in, expert_out, cotangent):
    tok_dev, columns = tokens.shape
    groups = lax.axis_size("expert")
    per_dev = expert_in.shape[0]
    experts = per_dev * groups
    capacity = 5 * tok_dev // (2 * experts)
    full_width = columns * groups
    slot_rows = per_dev * capacity
    slot_count = experts * capacity
    flat_routes = routes.reshape(-1)
    pairs_here = flat_routes.shape[0]
    places = jnp.arange(pairs_here, dtype=jnp.int32)
    same = flat_routes[:, None] == flat_routes[None, :]
    rank_in = jnp.sum((same & (places[None, :] < places[:, None])).astype(jnp.int32), axis=1)
    owner_idx = flat_routes // per_dev
    within = flat_routes % per_dev
    slot_ids = (within * capacity + rank_in) * groups + owner_idx
    placing = (slot_ids[:, None] == jnp.arange(slot_count, dtype=jnp.int32)[None, :]).astype(
        jnp.bfloat16
    )
    pair_gates = gate_values.reshape(-1)
    pair_tokens = jnp.repeat(tokens, 2, axis=0)
    cot_float = cotangent.astype(jnp.float32)
    pair_cot = (jnp.repeat(cot_float, 2, axis=0) * pair_gates[:, None]).astype(jnp.bfloat16)

    def to_slots(pairs):
        slots = jnp.einsum("ps,pc->sc", placing, pairs, preferred_element_type=jnp.float32)
        return slots.astype(jnp.bfloat16).reshape(slot_rows, groups, columns)

    def from_slots(back):
        return jnp.einsum(
            "ps,sc->pc",
            placing,
            back.reshape(slot_count, columns),
            preferred_element_type=jnp.float32,
        )

    def as_rows(gathered):
        return gathered.reshape(-1, per_dev, capacity, full_width)

    x_moved = lax.all_to_all(
        to_slots(pair_tokens), "expert", split_axis=1, concat_axis=1, tiled=True
    )
    x_rows = as_rows(
        lax.all_gather(x_moved.reshape(slot_rows, full_width), "dp", axis=0, tiled=True)
    )
    pre_act = jnp.einsum("bjcd,jdf->bjcf", x_rows, expert_in, preferred_element_type=jnp.float32)
    pre_act, hidden = (pre_act, gelu_tanh(pre_act).astype(jnp.bfloat16))
    part = hidden
    term = jnp.einsum("bjcf,jfd->bjcd", part, expert_out, preferred_element_type=jnp.float32)
    out_sum = lax.psum_scatter(
        term.reshape(lax.axis_size("dp") * slot_rows, full_width).astype(jnp.bfloat16),
        "dp",
        scatter_dimension=0,
        tiled=True,
    )
    out_back = lax.all_to_all(
        out_sum.reshape(slot_rows, groups, columns),
        "expert",
        split_axis=1,
        concat_axis=1,
        tiled=True,
    )
    dy_moved = lax.all_to_all(to_slots(pair_cot), "expert", split_axis=1, concat_axis=1, tiled=True)
    dy_rows = as_rows(
        lax.all_gather(dy_moved.reshape(slot_rows, full_width), "dp", axis=0, tiled=True)
    )
    d_hidden = jnp.einsum("bjcd,jfd->bjcf", dy_rows, expert_out, preferred_element_type=jnp.float32)
    backward_d_pre = jax.vjp(gelu_tanh, pre_act)[1](d_hidden)[0].astype(jnp.bfloat16)
    grad_out = jnp.einsum("bjcf,bjcd->jfd", hidden, dy_rows, preferred_element_type=jnp.float32)
    grad_in = jnp.einsum(
        "bjcd,bjcf->jdf", x_rows, backward_d_pre, preferred_element_type=jnp.float32
    )
    d_pre, grad_in, grad_out = (
        backward_d_pre,
        grad_in.astype(jnp.bfloat16),
        grad_out.astype(jnp.bfloat16),
    )
    part = d_pre
    term = jnp.einsum("bjcf,jdf->bjcd", part, expert_in, preferred_element_type=jnp.float32)
    dx_sum = lax.psum_scatter(
        term.reshape(lax.axis_size("dp") * slot_rows, full_width).astype(jnp.bfloat16),
        "dp",
        scatter_dimension=0,
        tiled=True,
    )
    dx_back = lax.all_to_all(
        dx_sum.reshape(slot_rows, groups, columns),
        "expert",
        split_axis=1,
        concat_axis=1,
        tiled=True,
    )
    out_view = from_slots(out_back).reshape(tok_dev, 2, columns)
    dx_view = from_slots(dx_back).reshape(tok_dev, 2, columns)
    gate_pairs = pair_gates.reshape(tok_dev, 2)
    layer_out = (out_view[:, 0] * gate_pairs[:, 0:1] + out_view[:, 1] * gate_pairs[:, 1:2]).astype(
        jnp.bfloat16
    )
    grad_tokens = (dx_view[:, 0] + dx_view[:, 1]).astype(jnp.bfloat16)
    gate_part = jnp.sum(cot_float[:, None, :] * out_view, axis=2)
    grad_gates = lax.psum(gate_part, "expert")
    return (layer_out, grad_tokens, grad_gates, grad_in, grad_out)


MESH = pl.DeviceIdType.MESH
BF16 = jnp.bfloat16
F32 = jnp.float32


def tiles_of(lo, hi, step=256):
    return [(at, min(at + step, hi)) for at in range(lo, hi, step)]


def dot(left, right, contract):
    return lax.dot_general(left, right, ((contract[:1], contract[1:]), ((), ())), preferred_element_type=F32)


def layer_kernel(
    tok_hbm, cot_hbm, routes_hbm, gates_hbm, w_in_hbm, w_out_hbm,
    out_ref, gtok_ref, gg_ref, gi, go,
    tok_ref, cot_ref, routes_t, gates_t,
    w_in, w_out, slots, zgot, own, rest, rows, hid, slope, dpre,
    term, mate, sums_r, relay_r, land_r, sums_w, relay_w, land_w, totals, zsend, zback, place, gpart,
    isem, wsem, a2a_s, a2a_r, own_s, own_r, rest_s, rest_r, mates_s, mates_r, rs_s, rs_r, rsw_s, rsw_r,
    back_s, back_r, gg_s, gg_r,
):
    cols, tok_dev = tok_ref.shape
    zs, per_dev, cap = slots.shape[1:4]
    width, hidden_here = w_in.shape[1:]
    head = own.shape[-1]
    experts = zs * per_dev
    z = lax.axis_index("expert")
    d = lax.axis_index("dp")
    core = d % 2
    xbit = (d // 2) % 2
    ybit = d // 4
    mate_d = d + 1 - 2 * core
    xn = d + 2 - 4 * xbit
    yn = d + 4 - 8 * ybit
    dd = xn + 4 - 8 * ybit
    first = core * yn + (1 - core) * xn
    second = core * xn + (1 - core) * yn

    def remote(src, dst, send, recv, zi, di):
        return pltpu.make_async_remote_copy(
            src_ref=src, dst_ref=dst, send_sem=send, recv_sem=recv, device_id=(zi, di), device_id_type=MESH
        )

    loads = [
        pltpu.make_async_copy(src, dst, isem.at[i])
        for i, (src, dst) in enumerate(
            ((routes_hbm, routes_t), (tok_hbm, tok_ref), (gates_hbm, gates_t), (cot_hbm, cot_ref))
        )
    ]
    for copy in loads:
        copy.start()
    barrier = pltpu.get_barrier_semaphore()
    for step in range(1, zs):
        pl.semaphore_signal(barrier, inc=1, device_id=((z + step) % zs, d), device_id_type=MESH)
    for other in (mate_d, xn, yn):
        pl.semaphore_signal(barrier, inc=1, device_id=(z, other), device_id_type=MESH)

    w_copies = []
    for j in range(per_dev):
        for i in range(zs):
            piece = pl.ds(pl.multiple_of(((z + i) % zs) * cols, 16), cols)
            w_copies.append(
                pltpu.make_async_copy(
                    w_in_hbm.at[j, piece], w_in.at[j, i * cols : (i + 1) * cols], wsem.at[j, i]
                )
            )
    for j in range(per_dev):
        w_copies.append(pltpu.make_async_copy(w_out_hbm.at[j], w_out.at[j], wsem.at[j, zs]))
    for copy in w_copies:
        copy.start()

    for copy in (loads[0], loads[2], loads[1], loads[3]):
        copy.wait()
    named = lax.broadcasted_iota(jnp.int32, (experts, tok_dev), 0)
    first_of = (named == routes_t[0:1, :]).astype(F32)
    second_of = (named == routes_t[1:2, :]).astype(F32)
    before = (
        lax.broadcasted_iota(jnp.int32, (tok_dev, tok_dev), 0)
        < lax.broadcasted_iota(jnp.int32, (tok_dev, tok_dev), 1)
    ).astype(F32).astype(BF16)
    earlier = dot((first_of + second_of).astype(BF16), before, (1, 0))
    slot_iota = lax.broadcasted_iota(jnp.int32, (experts * cap, tok_dev), 0)
    gate_col = jnp.zeros((experts * cap, 1), F32)
    for k, of in ((0, first_of), (1, second_of)):
        rank = jnp.sum(earlier * of, axis=0, keepdims=True).astype(jnp.int32)
        taken = (slot_iota == routes_t[k : k + 1, :] * cap + rank).astype(F32)
        place[k] = taken.astype(BF16)
        gate_col = gate_col + jnp.sum(taken * gates_t[k : k + 1, :], axis=1, keepdims=True)
    both = place[0] + place[1]
    by_slot = (zs, per_dev, cap, cols)

    a2a = [
        [
            [
                remote(
                    slots.at[a, (z + step) % zs, j], zgot.at[a, z, j],
                    a2a_s.at[a, j, step - 1], a2a_r.at[a, j, step - 1], (z + step) % zs, d,
                )
                for step in range(1, zs)
            ]
            for j in range(per_dev)
        ]
        for a in range(2)
    ]

    def exchange(a, j):
        for copy in a2a[a][j]:
            copy.start()

    def arrive(a, j):
        for copy in a2a[a][j]:
            copy.wait()

    def ag_copies(at, send, recv):
        made = []
        for i, (block, to) in enumerate(
            ((d, xn), (d, yn), (d, mate_d), (second, first), (xn, mate_d), (yn, mate_d), (dd, mate_d))
        ):
            made.append(remote(at(block), at(block), send.at[i], recv.at[i], z, to))
        return made

    ag_own = [ag_copies(lambda b, a=a: own.at[a, b], own_s.at[a], own_r.at[a]) for a in range(2)]
    ag_rest = [
        [
            ag_copies(lambda b, a=a, j=j: rest.at[a, j, b], rest_s.at[a, j], rest_r.at[a, j])
            for j in range(per_dev)
        ]
        for a in range(2)
    ]

    def own_start(a):
        own[a, pl.ds(d, 1)] = slots[a, pl.ds(z, 1), :, :, 0:head]
        for copy in ag_own[a][:3]:
            copy.start()

    def assemble(a, j):
        mine = slots[a, z, j].astype(F32)
        far = [zgot[a, (z + i) % zs, j].astype(F32) for i in range(1, zs)]
        whole = jnp.concatenate([mine[:, head:]] + far, axis=-1)
        rest[a, j, pl.ds(d, 1)] = whole.astype(BF16)[None]
        for copy in ag_rest[a][j][:3]:
            copy.start()

    def forward(copies):
        copies[0].wait_recv()
        copies[1].wait_recv()
        for i in (3, 4, 5):
            copies[i].start()

    def forward_last(copies):
        copies[3].wait_recv()
        copies[6].start()

    def landed_all(copies):
        for i in (2, 4, 5, 6):
            copies[i].wait_recv()

    chips = rows.shape[2] // (2 * cap)

    def finish(a, j, here):
        def pair(n, carry):
            half = n // (chips // 2)
            chip = (n % (chips // 2)) * 2
            blocks = []
            for b in (2 * chip + half, 2 * chip + 2 + half):
                whole = jnp.concatenate([own[a, b, j].astype(F32), rest[a, j, b].astype(F32)], axis=-1)
                if here:
                    turn = width - here * cols
                    whole = jnp.concatenate([whole[:, turn:], whole[:, :turn]], axis=-1)
                blocks.append(whole)
            at = pl.ds(pl.multiple_of(n * 2 * cap, 2 * cap), 2 * cap)
            rows[a, j, at, :] = jnp.concatenate(blocks, axis=0).astype(BF16)
            return carry

        lax.fori_loop(0, chips, pair, 0)

    def finish_x(j):
        landed_all(ag_rest[0][j])
        finish(0, j, 0)

    def finish_dy(j):
        landed_all(ag_rest[1][j])
        for here in range(zs):

            @pl.when(z == here)
            def _():
                finish(1, j, here)

    def activation(j, lo, hi):
        for start, end in tiles_of(lo, hi):
            v = dot(rows[0, j], w_in[j, :, start:end], (1, 0))
            scale = 0.7978845608028654
            sq = v * v
            t = jnp.tanh(scale * v * (1.0 + 0.044715 * sq))
            half = 0.5 * (1.0 + t)
            hid[j, :, start:end] = (v * half).astype(BF16)
            slope[j, :, start:end] = half + 0.5 * v * (1.0 - t * t) * (scale * (1.0 + 0.134145 * sq))

    def backward(j, lo, hi):
        for start, end in tiles_of(lo, hi):
            dh = dot(rows[1, j], w_out[j, start:end, :], (1, 1))
            dpre[j, :, start:end] = (slope[j, :, start:end] * dh).astype(BF16)

    def hops_of(sums, relay, land, send, recv):
        return [
            remote(src, land.at[i], send.at[i], recv.at[i], z, to)
            for i, (src, to) in enumerate(
                ((sums.at[dd // 2], first), (sums.at[first // 2], first), (relay, second))
            )
        ]

    swaps = [
        [
            remote(term.at[a, j, 1 - core], mate.at[a, j], mates_s.at[a, j], mates_r.at[a, j], z, mate_d)
            for j in range(per_dev)
        ]
        for a in range(2)
    ]
    others = sums_r.shape[-1]
    cut = 640
    spans = [[[(0, cut), (cut, others)] for j in range(per_dev)] for a in range(2)]

    def hops_at(a, j, k):
        lo, hi = spans[a][j][k]
        return hops_of(
            sums_r.at[a, j, :, :, lo:hi], relay_r.at[a, j, :, lo:hi], land_r.at[a, j, :, :, lo:hi],
            rs_s.at[a, j, k], rs_r.at[a, j, k],
        )

    hops_r = [[[hops_at(a, j, k) for k in range(len(spans[a][j]))] for j in range(per_dev)] for a in range(2)]
    hops_w = [
        hops_of(sums_w.at[a], relay_w.at[a], land_w.at[a], rsw_s.at[a], rsw_r.at[a]) for a in range(2)
    ]

    def terms(a, j, lo, hi):
        for start, end in tiles_of(lo, hi):
            if a == 0:
                v = dot(hid[j], w_out[j, :, start:end], (1, 0))
            else:
                v = dot(dpre[j], w_in[j, start:end, :], (1, 1))
            term[a, j, :, :, :, start:end] = v.reshape(2, chips, cap, end - start).astype(BF16)

    def swap(a, j):
        swaps[a][j].start()

    def split_sums(a, j, here):
        def chip(c, carry):
            total = term[a, j, core, c].astype(F32) + mate[a, j, c].astype(F32)
            if here:
                turn = here * cols
                total = jnp.concatenate([total[:, turn:], total[:, :turn]], axis=-1)
            sums_r[a, j, c] = total[:, head:].astype(BF16)
            sums_w[a, c, j] = total[:, :head].astype(BF16)
            return carry

        lax.fori_loop(0, chips, chip, 0)

    def sums(a, j):
        swaps[a][j].wait()
        if a == 1:
            split_sums(1, j, 0)
        else:
            for here in range(zs):

                @pl.when(z == here)
                def _():
                    split_sums(0, j, here)

        for hops in hops_r[a][j]:
            hops[0].start()
            hops[1].start()

    def own_hops(a):
        hops_w[a][0].start()
        hops_w[a][1].start()

    def pass_on(a, j, k):
        lo, hi = spans[a][j][k]
        hops_r[a][j][k][0].wait()
        both_ways = sums_r[a, j, second // 2, :, lo:hi].astype(F32) + land_r[a, j, 0, :, lo:hi].astype(F32)
        relay_r[a, j, :, lo:hi] = both_ways.astype(BF16)
        hops_r[a][j][k][2].start()

    def own_pass(a):
        hops_w[a][0].wait()
        relay_w[a] = (sums_w[a, second // 2].astype(F32) + land_w[a, 0].astype(F32)).astype(BF16)
        hops_w[a][2].start()

    back = [
        [
            [
                remote(
                    zsend.at[a, step - 1, j], zback.at[a, z, j],
                    back_s.at[a, j, step - 1], back_r.at[a, j, step - 1], (z + step) % zs, d,
                )
                for step in range(1, zs)
            ]
            for j in range(per_dev)
        ]
        for a in range(2)
    ]

    def end(a, j, k):
        lo, hi = spans[a][j][k]
        hops_r[a][j][k][1].wait()
        hops_r[a][j][k][2].wait()
        here = sums_r[a, j, d // 2, :, lo:hi].astype(F32)
        totals[a, j, :, lo:hi] = here + land_r[a, j, 1, :, lo:hi].astype(F32) + land_r[a, j, 2, :, lo:hi].astype(F32)
        tail = cols - head
        for i in range(zs - 1):
            start = tail + i * cols
            if lo < start + cols <= hi:
                zsend[a, i, j] = totals[a, j, :, start : start + cols].astype(BF16)
                back[a][j][i].start()

    def own_end(a):
        hops_w[a][1].wait()
        hops_w[a][2].wait()
        total = sums_w[a, d // 2].astype(F32) + land_w[a, 1].astype(F32) + land_w[a, 2].astype(F32)
        zback[a, pl.ds(z, 1)] = jnp.concatenate([total, totals[a, :, :, 0 : cols - head]], axis=-1).astype(BF16)[None]

    def weight_grad_out(j, lo, hi):
        for start, end in tiles_of(lo, hi):
            go[j, start:end, :] = dot(hid[j, :, start:end], rows[1, j], (0, 0)).astype(BF16)

    def weight_grad_in(j, lo, hi):
        for start, end in tiles_of(lo, hi):
            gi[j, start:end, :] = dot(rows[0, j, :, start:end], dpre[j], (0, 0)).astype(BF16)

    gg = []
    for step in range(1, zs):
        gg.append(
            remote(
                gpart.at[z], gpart.at[z], gg_s.at[step - 1], gg_r.at[step - 1], (z + step) % zs, d
            )
        )

    def views_of(a):
        slot_rows = zback[a].astype(F32).reshape(experts * cap, cols).astype(BF16)
        return [dot(slot_rows, place[k], (0, 0)) for k in range(2)]

    def combine_out():
        for j in range(per_dev):
            for copy in back[0][j]:
                copy.wait()
        views = views_of(0)
        out_ref[...] = (views[0] * gates_t[0:1, :] + views[1] * gates_t[1:2, :]).astype(BF16)
        cot = cot_ref[...].astype(F32)
        inner = [jnp.sum(cot * v, axis=0, keepdims=True) for v in views]
        row = lax.broadcasted_iota(jnp.int32, (8, tok_dev), 0)
        gpart[pl.ds(z, 1)] = jnp.where(row == 0, inner[0], inner[1])[None]
        for copy in gg:
            copy.start()

    def combine_tok():
        for j in range(per_dev):
            for copy in back[1][j]:
                copy.wait()
        views = views_of(1)
        gtok_ref[...] = (views[0] + views[1]).astype(BF16)

    def weights_in():
        for copy in w_copies:
            copy.wait()

    def grad_gates():
        for copy in gg:
            copy.wait()
        total = gpart[0] + gpart[1] + gpart[2] + gpart[3]
        gg_ref[...] = total[0:2]

    def place_dy():
        slots[1] = (dot(both, cot_ref[...], (1, 1)) * gate_col).reshape(by_slot).astype(BF16)

    slots[0] = dot(both, tok_ref[...], (1, 1)).reshape(by_slot).astype(BF16)
    pl.semaphore_wait(barrier, zs + 2)
    exchange(0, 0)
    own_start(0)
    exchange(0, 1)
    place_dy()
    own_start(1)
    forward(ag_own[0])
    arrive(0, 0)
    assemble(0, 0)
    exchange(1, 0)
    forward(ag_own[1])
    forward_last(ag_own[0])
    arrive(0, 1)
    assemble(0, 1)
    exchange(1, 1)
    forward_last(ag_own[1])
    forward(ag_rest[0][0])
    arrive(1, 0)
    assemble(1, 0)
    forward(ag_rest[0][1])
    forward_last(ag_rest[0][0])
    weights_in()
    landed_all(ag_own[0])
    finish_x(0)
    activation(0, 0, 256)
    arrive(1, 1)
    assemble(1, 1)
    activation(0, 256, hidden_here)
    forward_last(ag_rest[0][1])
    forward(ag_rest[1][0])
    terms(0, 0, 0, width)
    swap(0, 0)
    finish_x(1)
    activation(1, 0, 512)
    forward(ag_rest[1][1])
    forward_last(ag_rest[1][0])
    sums(0, 0)
    activation(1, 512, hidden_here)
    terms(0, 1, 0, width)
    swap(0, 1)
    forward_last(ag_rest[1][1])
    landed_all(ag_own[1])
    finish_dy(0)
    backward(0, 0, hidden_here)
    sums(0, 1)
    own_hops(0)
    pass_on(0, 0, 0)
    pass_on(0, 0, 1)
    terms(1, 0, 0, width)
    swap(1, 0)
    finish_dy(1)
    backward(1, 0, hidden_here)
    sums(1, 0)
    terms(1, 1, 0, width)
    swap(1, 1)
    pass_on(0, 1, 0)
    pass_on(0, 1, 1)
    own_pass(0)
    end(0, 0, 0)
    end(0, 0, 1)
    weight_grad_out(0, 0, 512)
    sums(1, 1)
    end(0, 1, 0)
    end(0, 1, 1)
    own_end(0)
    weight_grad_out(0, 512, hidden_here)
    pass_on(1, 0, 0)
    pass_on(1, 0, 1)
    weight_grad_out(1, 0, 512)
    pass_on(1, 1, 0)
    pass_on(1, 1, 1)
    own_hops(1)
    weight_grad_out(1, 512, hidden_here)
    end(1, 0, 0)
    end(1, 0, 1)
    own_pass(1)
    combine_out()
    end(1, 1, 0)
    end(1, 1, 1)
    weight_grad_in(0, 0, width)
    weight_grad_in(1, 0, width)
    own_end(1)
    grad_gates()
    combine_tok()
    for a in range(2):
        for copy in ag_own[a]:
            copy.wait_send()
        for j in range(per_dev):
            for copy in ag_rest[a][j]:
                copy.wait_send()


def store_kernel(out_in, gtok_in, gg_in, gi, go, out_hbm, gtok_hbm, gg_hbm, gi_hbm, go_hbm, sem, wsem):
    per_dev, width, _ = gi.shape
    zs = wsem.shape[1] - 1
    cols = width // zs
    z = lax.axis_index("expert")
    copies = []
    for j in range(per_dev):
        copies.append(pltpu.make_async_copy(go.at[j], go_hbm.at[j], wsem.at[j, zs]))
        for i in range(zs):
            piece = pl.ds(pl.multiple_of(((z + i) % zs) * cols, 16), cols)
            copies.append(
                pltpu.make_async_copy(gi.at[j, i * cols : (i + 1) * cols], gi_hbm.at[j, piece], wsem.at[j, i])
            )
    for i, (here, there) in enumerate(((out_in, out_hbm), (gtok_in, gtok_hbm), (gg_in, gg_hbm))):
        copies.append(pltpu.make_async_copy(here, there, sem.at[i]))
    for copy in copies:
        copy.start()
    for copy in copies:
        copy.wait()


def fused_shards(tokens, routes, gate_values, expert_in, expert_out, cotangent):
    tok_dev, cols = tokens.shape
    zs = lax.axis_size("expert")
    dps = lax.axis_size("dp")
    per_dev, width, hidden_here = expert_in.shape
    experts = per_dev * zs
    cap = 5 * tok_dev // (2 * experts)
    all_rows = dps * cap
    head = cols // 128 * 128
    others = width - head
    chips = dps // 2
    vmem = pl.BlockSpec(memory_space=pltpu.VMEM)
    hbm = pl.BlockSpec(memory_space=pl.ANY)
    dma = pltpu.SemaphoreType.DMA

    results = pl.pallas_call(
        layer_kernel,
        out_shape=(
            pltpu.VMEM((cols, tok_dev), BF16),
            pltpu.VMEM((cols, tok_dev), BF16),
            pltpu.VMEM((2, tok_dev), F32),
            pltpu.VMEM(expert_in.shape, BF16),
            pltpu.VMEM(expert_out.shape, BF16),
        ),
        in_specs=[hbm] * 6,
        out_specs=(vmem,) * 5,
        scratch_shapes=[
            pltpu.VMEM((cols, tok_dev), BF16),
            pltpu.VMEM((cols, tok_dev), BF16),
            pltpu.VMEM((2, tok_dev), jnp.int32),
            pltpu.VMEM((2, tok_dev), F32),
            pltpu.VMEM(expert_in.shape, BF16),
            pltpu.VMEM(expert_out.shape, BF16),
            pltpu.VMEM((2, zs, per_dev, cap, cols), BF16),
            pltpu.VMEM((2, zs, per_dev, cap, cols), BF16),
            pltpu.VMEM((2, dps, per_dev, cap, head), BF16),
            pltpu.VMEM((2, per_dev, dps, cap, others), BF16),
            pltpu.VMEM((2, per_dev, all_rows, width), BF16),
            pltpu.VMEM((per_dev, all_rows, hidden_here), BF16),
            pltpu.VMEM((per_dev, all_rows, hidden_here), F32),
            pltpu.VMEM((per_dev, all_rows, hidden_here), BF16),
            pltpu.VMEM((2, per_dev, 2, chips, cap, width), BF16),
            pltpu.VMEM((2, per_dev, chips, cap, width), BF16),
            pltpu.VMEM((2, per_dev, chips, cap, others), BF16),
            pltpu.VMEM((2, per_dev, cap, others), BF16),
            pltpu.VMEM((2, per_dev, 3, cap, others), BF16),
            pltpu.VMEM((2, chips, per_dev, cap, head), BF16),
            pltpu.VMEM((2, per_dev, cap, head), BF16),
            pltpu.VMEM((2, 3, per_dev, cap, head), BF16),
            pltpu.VMEM((2, per_dev, cap, others), F32),
            pltpu.VMEM((2, zs - 1, per_dev, cap, cols), BF16),
            pltpu.VMEM((2, zs, per_dev, cap, cols), BF16),
            pltpu.VMEM((2, experts * cap, tok_dev), BF16),
            pltpu.VMEM((zs, 8, tok_dev), F32),
            dma((4,)),
            dma((per_dev, zs + 1)),
            dma((2, per_dev, zs - 1)), dma((2, per_dev, zs - 1)),
            dma((2, 7)), dma((2, 7)),
            dma((2, per_dev, 7)), dma((2, per_dev, 7)),
            dma((2, per_dev)), dma((2, per_dev)),
            dma((2, per_dev, 2, 3)), dma((2, per_dev, 2, 3)),
            dma((2, 3)), dma((2, 3)),
            dma((2, per_dev, zs - 1)), dma((2, per_dev, zs - 1)),
            dma((zs - 1,)), dma((zs - 1,)),
        ],
        compiler_params=pltpu.CompilerParams(
            collective_id=0, has_side_effects=True, vmem_limit_bytes=48 * 1024 * 1024
        ),
    )(tokens.T, cotangent.T, routes.T, gate_values.T, expert_in, expert_out)
    layer_t, gtok_t, gates_grad_t, grad_in, grad_out = pl.pallas_call(
        store_kernel,
        out_shape=(
            jax.ShapeDtypeStruct((cols, tok_dev), BF16),
            jax.ShapeDtypeStruct((cols, tok_dev), BF16),
            jax.ShapeDtypeStruct((2, tok_dev), F32),
            jax.ShapeDtypeStruct(expert_in.shape, BF16),
            jax.ShapeDtypeStruct(expert_out.shape, BF16),
        ),
        in_specs=[vmem] * 5,
        out_specs=(hbm,) * 5,
        scratch_shapes=[dma((3,)), dma((per_dev, zs + 1))],
        compiler_params=pltpu.CompilerParams(vmem_limit_bytes=1024 * 1024),
    )(*results)
    return (layer_t.T, gtok_t.T, gates_grad_t.T, grad_in, grad_out)


def solution(mesh):
    placed = (
        P("dp", "expert"),
        P("dp", None),
        P("dp", None),
        P("expert", None, "dp"),
        P("expert", "dp", None),
        P("dp", "expert"),
    )
    fused = mesh.shape["expert"] == 4 and mesh.shape["dp"] == 8
    return jax.shard_map(
        fused_shards if fused else shards,
        mesh=mesh,
        in_specs=placed,
        out_specs=(
            P("dp", "expert"),
            P("dp", "expert"),
            P("dp", None),
            P("expert", None, "dp"),
            P("expert", "dp", None),
        ),
        check_vma=False,
    )
```
